32 devices in a mesh: gx: 8 (over y, x, core), gy: 4 (over z).
Axes of the slice: x: 2, y: 2, z: 4, core: 2. Of those that a mesh axis runs over, the one named last changes fastest.
Arguments:
- basis_vec: float32 [16, 128, 1024], P(None, 'gx', 'gy'), may hold values from -6 to 6
- conductivity: float32 [16, 128, 1024], P(None, 'gx', 'gy'), may hold values from 0.2 to 5
- sign_vals: int32 [128, 1024], P('gx', 'gy'), may hold values from -1 to 1, as said below
- sample_cols: int32 [64], P('gy'), may hold values from 0 to 255, as said below
Outputs:
- precond: float32 [16, 128, 1024], P(None, 'gx', 'gy')
- image_vec: float32 [16, 128, 1024], P(None, 'gx', 'gy')
- sketch: float32 [16, 128, 16], P(None, 'gx')
The draws below stay inside these ranges and needn't reach their ends.
Inputs may be any that keep to these rules, and one draw needn't show every extreme that they name: `sign_vals`: each entry is -1 or 1. `sample_cols`: the entries of each aligned block of 16 are distinct column offsets within one block of 256 columns.
All inputs are finite; a program needn't handle non-finite values.
Results may differ from the reference program's by a relative error of at most 0.0002.
Values sent between devices are 32-bit elements; how exact they have to be, the bound alone decides.
No kernel may reach another device: no remote copies, remote signals or barrier semaphores. Data moves between devices by JAX's collectives and lax.ppermute only.
A program may use at most 64 MiB of HBM per device.

```python
import math
import jax
import jax.numpy as jnp
from jax import lax

DEPTH = 16
CX = 16
CY = 256
SWEEPS = 8
SAMPLES = 16
NX = 128
NY = 1024
N_GX = 8
N_GY = 4


def draw_sign_vals(key, part):
    return (2 * jax.random.randint(key, (NX, NY), 0, 2) - 1).astype(jnp.int32)


def draw_sample_cols(key, part):
    block_keys = jax.random.split(jax.random.fold_in(key, 7), NY // CY)

    def one_block(block_key):
        key_pick, key_mix = jax.random.split(block_key)
        middle_cols = jax.random.permutation(key_pick, CY - 2)[:SAMPLES - 2] + 1
        chosen = jnp.concatenate([jnp.array([0, CY - 1], jnp.int32), middle_cols.astype(jnp.int32)])
        return jax.random.permutation(key_mix, chosen)
    return jax.vmap(one_block)(block_keys).reshape(-1).astype(jnp.int32)


def levels(own_key, shape, cuts, least, top_value):
    level, own = 1.0, jax.random.fold_in(own_key, 6)
    for axis_at, blocks in cuts:
        steps = jnp.exp(jax.random.uniform(jax.random.fold_in(own, axis_at), (blocks,), jnp.float32, least / len(cuts), top_value / len(cuts)))
        level = level * jnp.repeat(steps, shape[axis_at] // blocks).reshape([-1 if axis == axis_at else 1 for axis in range(len(shape))])
    return level


def bell_draw(own_key, dims, width, reach, shards=(), kind=jnp.bfloat16):
    drawn = width * jax.random.normal(own_key, dims, jnp.float32)
    if shards:
        drawn = drawn * levels(own_key, dims, shards, -0.22, 0.18)
    return jnp.clip(drawn, -reach, reach).astype(kind)


def setup_inputs(seed: int = 0) -> dict:
    splits = jax.random.split(jax.random.key(seed), 5)
    return {
        "basis_vec": bell_draw(splits[0], (DEPTH, NX, NY), 1.0, 6.0, ((1, 8), (2, 4)), jnp.float32),
        "conductivity": jnp.clip(jnp.exp(math.log(5.0) - 3.218876 * jax.random.uniform(splits[1], (DEPTH, NX, NY), jnp.float32) ** levels(splits[1], (DEPTH, NX, NY), ((1, 8), (2, 4)), -0.2, 0.2)), 0.2, 5.0),
        "sign_vals": draw_sign_vals(jax.random.fold_in(splits[4], 71), 0),
        "sample_cols": draw_sample_cols(jax.random.fold_in(splits[4], 71), 0),
    }


reaction = 0.5
lowest = 0.5
highest = 62.0

def operate(values, conduct):
    padded = jnp.pad(values, ((1, 1), (0, 0), (0, 0)))
    centre_val = padded[1:-1, 1:-1, 1:-1]
    kappa_mid = conduct[1:-1, 1:-1, 1:-1]
    neighbours = ((padded[2:, 1:-1, 1:-1], conduct[2:, 1:-1, 1:-1]), (padded[:-2, 1:-1, 1:-1], conduct[:-2, 1:-1, 1:-1]), (padded[1:-1, 2:, 1:-1], conduct[1:-1, 2:, 1:-1]), (padded[1:-1, :-2, 1:-1], conduct[1:-1, :-2, 1:-1]), (padded[1:-1, 1:-1, 2:], conduct[1:-1, 1:-1, 2:]), (padded[1:-1, 1:-1, :-2], conduct[1:-1, 1:-1, :-2]))
    summed = reaction * centre_val
    for near_value, near_kappa in neighbours:
        summed = summed + 0.5 * (kappa_mid + near_kappa) * (centre_val - near_value)
    return summed

def hartley_table(length):
    row_ids = jnp.arange(length, dtype=jnp.int32)[:, None]
    col_ids = jnp.arange(length, dtype=jnp.int32)[None, :]
    angles = (row_ids * col_ids % length).astype(jnp.float32) * (2.0 * jnp.pi / length)
    return (jnp.cos(angles) + jnp.sin(angles)) / jnp.sqrt(jnp.float32(length))

def walsh_table(length):
    row_ids = jnp.arange(length, dtype=jnp.int32)[:, None]
    col_ids = jnp.arange(length, dtype=jnp.int32)[None, :]
    parity = jnp.zeros((length, length), jnp.int32)
    for shift_no in range(length.bit_length() - 1):
        parity = parity + (row_ids >> shift_no & 1) * (col_ids >> shift_no & 1)
    return (1 - 2 * (parity % 2)).astype(jnp.float32) / jnp.sqrt(jnp.float32(length))

def reference(basis_vec, conductivity, sign_vals, sample_cols):
    conduct = jnp.pad(conductivity, 1)

    def apply_grid(values):
        return operate(jnp.pad(values, ((0, 0), (1, 1), (1, 1))), conduct)
    middle = (highest + lowest) / 2.0
    spread = (highest - lowest) / 2.0
    sig_ratio = middle / spread
    rho_now = 1.0 / sig_ratio
    residual = basis_vec
    direction = residual * (1.0 / middle)
    precond = jnp.zeros_like(basis_vec)
    for sweep_no in range(SWEEPS):
        precond = precond + direction
        if sweep_no < SWEEPS - 1:
            residual = residual - apply_grid(direction)
            rho_next = 1.0 / (2.0 * sig_ratio - rho_now)
            direction = rho_next * rho_now * direction + 2.0 * rho_next / spread * residual
            rho_now = rho_next
    image_vec = apply_grid(precond)
    flipped = image_vec * sign_vals.astype(jnp.float32)[None]
    blocks = flipped.reshape(DEPTH, N_GX, CX, NY)
    mixed_vec = jnp.einsum('jk,dgkc->dgjc', hartley_table(CX), blocks, precision=lax.Precision.HIGHEST)
    mixed_vec = jnp.einsum('hg,dgjc->dhjc', walsh_table(N_GX), mixed_vec, precision=lax.Precision.HIGHEST)
    mixed_vec = mixed_vec.reshape(DEPTH, NX, NY)
    global_cols = sample_cols.reshape(N_GY, SAMPLES) + (jnp.arange(N_GY, dtype=jnp.int32) * CY)[:, None]
    picked = jnp.take(mixed_vec, global_cols.reshape(-1).astype(jnp.int32), axis=2)
    sketch = lax.optimization_barrier(jnp.sum(picked.reshape(DEPTH, NX, N_GY, SAMPLES), axis=2))
    return (precond, image_vec, sketch)
```

```python
import jax
import jax.numpy as jnp
import numpy as np
from jax import lax
from jax.experimental import pallas as pl
from jax.experimental.pallas import tpu as pltpu
from jax.sharding import PartitionSpec as P

SWEEPS = 8
reaction = 0.5
lowest = 0.5
highest = 62.0
HALO = SWEEPS
LANES = 128
AXES = ("gx", "gy")


def even_pair(i, n):
    return i ^ 1


def odd_pair(i, n):
    j = ((i + 1) ^ 1) - 1
    return j if 0 <= j < n else None


def same(i, n):
    return i


def exchange(array, row_map, col_map):
    rows, cols = lax.axis_size("gx"), lax.axis_size("gy")
    pairs = []
    for g in range(rows):
        for y in range(cols):
            to_g, to_y = row_map(g, rows), col_map(y, cols)
            if to_g is not None and to_y is not None:
                pairs.append((g * cols + y, to_g * cols + to_y))
    return lax.ppermute(array, AXES, pairs)


def swap(array, axis, mask):
    return lax.ppermute(array, axis, [(i, i ^ mask) for i in range(lax.axis_size(axis))])


def bit_groups(bits):
    return [bits[i : i + 2] for i in range(0, len(bits), 2)]


def masks_of(group):
    masks = [0]
    for bit in group:
        masks = masks + [m | 1 << bit for m in masks]
    return masks


def walsh_sign(index, mask, group):
    parity = jnp.int32(0)
    for bit in group:
        parity = parity + (index >> bit & (index ^ mask) >> bit & 1)
    return (1 - 2 * (parity & 1)).astype(jnp.float32)


def hartley_mix(depth, rows, scale):
    angles = (np.outer(np.arange(rows), np.arange(rows)) % rows) * (2.0 * np.pi / rows)
    table = (np.cos(angles) + np.sin(angles)) / np.sqrt(rows) * scale
    mixed = np.einsum("jk,de->kdej", table, np.eye(depth))
    return mixed.reshape(rows * depth, depth * rows).astype(np.float32)


def split_lanes(source, tiles):
    for t in range(tiles.shape[0]):
        tiles[t] = source[:, t * LANES : (t + 1) * LANES]


def take_row(tiles, row, depth, rows):
    picked = [tiles[t, pl.ds(row, depth, stride=rows), :] for t in range(tiles.shape[0])]
    return jnp.concatenate(picked, axis=1)


def put_row(tiles, row, slab, depth, rows):
    for t in range(tiles.shape[0]):
        tiles[t, pl.ds(row, depth, stride=rows), :] = slab[:, t * LANES : (t + 1) * LANES]


def join_lanes(tiles, target):
    for t in range(tiles.shape[0]):
        target[:, t * LANES : (t + 1) * LANES] = tiles[t]


def pack_kernel(flags, basis, cond, top_rows, bottom_rows, left, right, tiles, *, depth, rows, cols):
    odd = flags[0] == 1
    lane = lax.broadcasted_iota(jnp.int32, (depth, LANES), 1)
    for a, source in enumerate((basis, cond)):
        lo = jnp.zeros((depth, LANES), jnp.float32)
        hi = jnp.zeros((depth, LANES), jnp.float32)
        slabs = []
        split_lanes(source, tiles.at[a])
        for r in range(rows):
            slab = take_row(tiles.at[a], r, depth, rows)
            slabs.append(slab)
            mine = (lane >= r * HALO) & (lane < (r + 1) * HALO)
            first = slab[:, :LANES]
            last = slab[:, cols - LANES :]
            lo = jnp.where(mine, pltpu.roll(first, r * HALO, 1) if r else first, lo)
            hi = jnp.where(mine, pltpu.roll(last, (r + 1) * HALO % LANES, 1) if (r + 1) * HALO % LANES else last, hi)
        for r in range(HALO):
            up, down = slabs[r], slabs[rows - HALO + r]
            top_rows[a, r] = jnp.where(odd, down, up)
            bottom_rows[a, r] = jnp.where(odd, up, down)
        col_odd = flags[1] == 1
        left[a] = jnp.where(col_odd, hi, lo)
        right[a] = jnp.where(col_odd, lo, hi)


def main_kernel(flags, basis, cond, rows_odd, rows_even, strip_odd, strip_even, corner_odd, corner_even,
                signs, picks, mix, precond_out, image_out, sketch_out,
                res, dirn, pre, kx, ky, kz, diag, flip, tiles, *, depth, rows, cols, samples):
    width = cols + LANES
    span = rows + 2 * HALO
    odd = flags[0] == 1
    col_odd = flags[1] == 1
    top, bottom, left, right = (flags[i].astype(jnp.float32) for i in range(2, 6))
    middle = (highest + lowest) / 2.0
    spread = (highest - lowest) / 2.0
    lane = lax.broadcasted_iota(jnp.int32, (depth, LANES), 1)
    tail = (lane < HALO, lane >= LANES - HALO)

    def side_lanes(strips, at):
        lo, hi = strips
        shift_hi = (LANES - at * HALO) % LANES
        shift_lo = (2 * LANES - HALO - at * HALO) % LANES
        hi = pltpu.roll(hi, shift_hi, 1) if shift_hi else hi
        lo = pltpu.roll(lo, shift_lo, 1) if shift_lo else lo
        return jnp.where(tail[0], hi, jnp.where(tail[1], lo, 0.0))

    def ordered(strip_o, strip_e):
        return jnp.where(col_odd, strip_e, strip_o), jnp.where(col_odd, strip_o, strip_e)

    for a, (source, target) in enumerate(((basis, res), (cond, pre))):
        split_lanes(source, tiles.at[a])
        own = ordered(strip_odd[a], strip_even[a])
        far_odd = ordered(corner_odd[0, a], corner_odd[1, a])
        far_even = ordered(corner_even[0, a], corner_even[1, a])
        above = tuple(jnp.where(odd, e, o) for o, e in zip(far_odd, far_even))
        below = tuple(jnp.where(odd, o, e) for o, e in zip(far_odd, far_even))
        for j in range(span):
            if j < HALO:
                slab = jnp.where(odd, rows_even[a, j], rows_odd[a, j])
                side = side_lanes(above, rows - HALO + j)
            elif j < HALO + rows:
                slab = take_row(tiles.at[a], j - HALO, depth, rows)
                side = side_lanes(own, j - HALO)
            else:
                slab = jnp.where(odd, rows_odd[a, j - HALO - rows], rows_even[a, j - HALO - rows])
                side = side_lanes(below, j - HALO - rows)
            target[j, :, :cols] = slab
            target[j, :, cols:] = side

    def back(x, axis):
        return pltpu.roll(x, 1, axis)

    def ahead(x, axis):
        return pltpu.roll(x, x.shape[axis] - 1, axis)

    deep = lax.broadcasted_iota(jnp.int32, (depth, width), 0)
    wide = lax.broadcasted_iota(jnp.int32, (depth, width), 1)
    z_ends = (deep == 0).astype(jnp.float32) + (deep == depth - 1).astype(jnp.float32)
    z_inner = (deep < depth - 1).astype(jnp.float32)
    ends = z_ends + left * (wide == 0).astype(jnp.float32) + right * (wide == cols - 1).astype(jnp.float32)
    x_inner = 1.0 - right * (wide == cols - 1).astype(jnp.float32) - left * (wide == width - 1).astype(jnp.float32)

    def faces(j, here):
        half = 0.5 * here
        kx[j] = (half + ahead(half, 1)) * x_inner
        kz[j] = (half + ahead(half, 0)) * z_inner
        at_edge = jnp.where(j == HALO, top, 0.0) + jnp.where(j == HALO + rows - 1, bottom, 0.0)
        diag[j] = reaction + half * (ends + at_edge)
        dirn[j] = res[j] * (1.0 / middle)
        nxt = pre[j + 1]
        open_face = 1.0 - jnp.where(j == HALO - 1, top, 0.0) - jnp.where(j == HALO + rows - 1, bottom, 0.0)
        ky[j] = (half + 0.5 * nxt) * open_face
        return nxt

    kappa = lax.fori_loop(0, span - 1, faces, pre[0])
    dirn[span - 1] = res[span - 1] * (1.0 / middle)

    def sweep(low, high, field, emit):
        start = field[low]
        before = field[low - 1]

        def body(j, carry):
            here, flux_y = carry
            nxt = field[j + 1]
            flux = ky[j] * (here - nxt)
            flux_x = kx[j] * (here - ahead(here, 1))
            flux_z = kz[j] * (here - ahead(here, 0))
            applied = diag[j] * here + (flux - flux_y) + (flux_x - back(flux_x, 1)) + (flux_z - back(flux_z, 0))
            emit(j, here, applied)
            return nxt, flux

        lax.fori_loop(low, high, body, (start, ky[low - 1] * (before - start)), unroll=2)

    sig_ratio = middle / spread
    rho_now = 1.0 / sig_ratio

    def begin(j, _):
        pre[j] = dirn[j]
        return 0

    lax.fori_loop(0, span, begin, 0)
    for step in range(1, SWEEPS):
        rho_next = 1.0 / (2.0 * sig_ratio - rho_now)
        keep, gain = rho_next * rho_now, 2.0 * rho_next / spread
        rho_now = rho_next

        def emit(j, here, applied):
            left_over = res[j] - applied
            res[j] = left_over
            fresh = keep * here + gain * left_over
            dirn[j] = fresh
            pre[j] = pre[j] + fresh

        sweep(step, span - step, dirn, emit)

    def finish(j, here, applied):
        row = j - HALO
        image = applied[:, :cols]
        put_row(tiles.at[0], row, here[:, :cols], depth, rows)
        put_row(tiles.at[1], row, image, depth, rows)
        flip[pl.ds(pl.multiple_of(row * depth, depth), depth), :] = image * signs[pl.ds(row, 1), :].astype(jnp.float32)

    sweep(HALO, HALO + rows, pre, finish)
    join_lanes(tiles.at[0], precond_out)
    join_lanes(tiles.at[1], image_out)
    col_ids = lax.broadcasted_iota(jnp.int32, (samples, cols), 1)
    chosen = (picks[...] == col_ids).astype(jnp.float32)
    picked = lax.dot_general(chosen, flip[...], (((1,), (1,)), ((), ())),
                             precision=lax.Precision.HIGHEST, preferred_element_type=jnp.float32)
    sketch_out[...] = lax.dot_general(picked, mix[...], (((1,), (0,)), ((), ())),
                                      precision=lax.Precision.HIGHEST, preferred_element_type=jnp.float32)


def per_device(basis_vec, conductivity, sign_vals, sample_cols):
    depth, rows, cols = basis_vec.shape
    samples = sample_cols.shape[0]
    gx_size, gy_size = lax.axis_size("gx"), lax.axis_size("gy")
    gx_index, gy_index = lax.axis_index("gx"), lax.axis_index("gy")
    flags = jnp.stack([
        gx_index & 1, gy_index & 1, gx_index == 0, gx_index == gx_size - 1, gy_index == 0, gy_index == gy_size - 1,
    ]).astype(jnp.int32)
    basis = basis_vec.reshape(depth * rows, cols)
    cond = conductivity.reshape(depth * rows, cols)
    smem = pl.BlockSpec(memory_space=pltpu.SMEM)
    vmem = pl.BlockSpec(memory_space=pltpu.VMEM)
    sizes = dict(depth=depth, rows=rows, cols=cols)
    f32 = jnp.float32
    row_msg = jax.ShapeDtypeStruct((2, HALO, depth, cols), f32)
    strip_msg = jax.ShapeDtypeStruct((2, depth, LANES), f32)
    to_odd, to_even, strip_to_odd, strip_to_even = pl.pallas_call(
        lambda *refs: pack_kernel(*refs, **sizes),
        in_specs=[smem, vmem, vmem],
        out_specs=[vmem] * 4,
        out_shape=[row_msg, row_msg, strip_msg, strip_msg],
        scratch_shapes=[pltpu.VMEM((2, cols // LANES, depth * rows, LANES), f32)],
        name="pack",
    )(flags, basis, cond)
    with jax.named_scope("rows_odd"):
        rows_odd = exchange(to_odd, odd_pair, same)
    with jax.named_scope("strip_odd"):
        strip_odd = exchange(strip_to_odd, same, odd_pair)
    with jax.named_scope("strip_even"):
        strip_even = exchange(strip_to_even, same, even_pair)
    with jax.named_scope("rows_even"):
        rows_even = exchange(to_even, even_pair, same)
    strips = jnp.stack([strip_odd, strip_even])
    with jax.named_scope("corner_odd"):
        corner_odd = exchange(strips, odd_pair, same)
    with jax.named_scope("corner_even"):
        corner_even = exchange(strips, even_pair, same)
    mix = jnp.asarray(hartley_mix(depth, rows, 1.0 / np.sqrt(gx_size)))
    span, width = rows + 2 * HALO, cols + LANES
    precond, image, current = pl.pallas_call(
        lambda *refs: main_kernel(*refs, samples=samples, **sizes),
        in_specs=[smem] + [vmem] * 11,
        out_specs=[vmem] * 3,
        out_shape=[jax.ShapeDtypeStruct((depth * rows, cols), f32)] * 2
        + [jax.ShapeDtypeStruct((samples, depth * rows), f32)],
        scratch_shapes=[pltpu.VMEM((span, depth, width), f32)] * 7 + [
            pltpu.VMEM((depth * rows, cols), f32),
            pltpu.VMEM((2, cols // LANES, depth * rows, LANES), f32),
        ],
        name="solve",
    )(flags, basis, cond, rows_odd, rows_even, strip_odd, strip_even, corner_odd, corner_even,
      sign_vals, sample_cols.reshape(samples, 1), mix)
    gx_bits = gx_size.bit_length() - 1
    for group in [[0]] + bit_groups(list(range(1, gx_bits))):
        total = walsh_sign(gx_index, 0, group) * current
        for mask in masks_of(group)[1:]:
            total = total + walsh_sign(gx_index, mask, group) * swap(current, "gx", mask)
        current = total
    for group in bit_groups(list(range(gy_size.bit_length() - 1))):
        current = current + sum(swap(current, "gy", mask) for mask in masks_of(group)[1:])
    shape = (depth, rows, cols)
    sketch = current.T.reshape(depth, rows, samples)
    return precond.reshape(shape), image.reshape(shape), sketch


def solution(mesh):
    in_specs = (P(None, "gx", "gy"), P(None, "gx", "gy"), P("gx", "gy"), P("gy"))
    out_specs = (P(None, "gx", "gy"), P(None, "gx", "gy"), P(None, "gx", None))
    return jax.shard_map(
        per_device, mesh=mesh, in_specs=in_specs, out_specs=out_specs, check_vma=False
    )
```

```python
import jax
import jax.numpy as jnp
import numpy as np
from jax import lax
from jax.experimental import pallas as pl
from jax.experimental.pallas import tpu as pltpu
from jax.sharding import PartitionSpec as P

SWEEPS = 8
reaction = 0.5
lowest = 0.5
highest = 62.0
HALO = SWEEPS
LANES = 128
AXES = ("gx", "gy")


def even_pair(i, n):
    return i ^ 1


def odd_pair(i, n):
    j = ((i + 1) ^ 1) - 1
    return j if 0 <= j < n else None


def same(i, n):
    return i


def exchange(array, row_map, col_map):
    rows, cols = lax.axis_size("gx"), lax.axis_size("gy")
    pairs = []
    for g in range(rows):
        for y in range(cols):
            to_g, to_y = row_map(g, rows), col_map(y, cols)
            if to_g is not None and to_y is not None:
                pairs.append((g * cols + y, to_g * cols + to_y))
    return lax.ppermute(array, AXES, pairs)


def swap(array, axis, mask):
    return lax.ppermute(array, axis, [(i, i ^ mask) for i in range(lax.axis_size(axis))])


def bit_groups(bits):
    return [bits[i : i + 2] for i in range(0, len(bits), 2)]


def masks_of(group):
    masks = [0]
    for bit in group:
        masks = masks + [m | 1 << bit for m in masks]
    return masks


def walsh_sign(index, mask, group):
    parity = jnp.int32(0)
    for bit in group:
        parity = parity + (index >> bit & (index ^ mask) >> bit & 1)
    return (1 - 2 * (parity & 1)).astype(jnp.float32)


def hartley_mix(depth, rows, scale):
    angles = (np.outer(np.arange(rows), np.arange(rows)) % rows) * (2.0 * np.pi / rows)
    table = (np.cos(angles) + np.sin(angles)) / np.sqrt(rows) * scale
    return np.kron(np.eye(depth), table.T).astype(np.float32)


def turn(tiles):
    count = len(tiles)
    sub = lax.broadcasted_iota(jnp.int32, tiles[0].shape, 0)
    tiles = list(tiles)
    step = 1
    while step < count:
        low = (sub & step) == 0
        for i in range(count):
            if not i & step:
                a, b = tiles[i], tiles[i + step]
                tiles[i] = jnp.where(low, a, pltpu.roll(b, step, 0))
                tiles[i + step] = jnp.where(low, pltpu.roll(a, count - step, 0), b)
        step *= 2
    return tiles


def pack_kernel(flags, basis, cond, to_odd, to_even, left, right, *, depth, rows, cols):
    odd, col_odd = flags[0] == 1, flags[1] == 1
    half = depth // 2
    lane = lax.broadcasted_iota(jnp.int32, (half, LANES), 1)
    for a, source in enumerate((basis, cond)):
        for t in range(2):
            part = slice(t * half, (t + 1) * half)
            lo = hi = jnp.zeros((half, LANES), jnp.float32)
            for c in range(cols // LANES):
                span = slice(c * LANES, (c + 1) * LANES)
                slabs = []
                for r in range(0, rows, half):
                    slabs += turn([source[2 * s + t, r : r + half, span] for s in range(half)])
                for r in range(HALO):
                    first, last = slabs[r], slabs[rows - HALO + r]
                    to_odd[a, r, part, span] = jnp.where(odd, last, first)
                    to_even[a, r, part, span] = jnp.where(odd, first, last)
                for r in range(rows):
                    mine = (lane >= r * HALO) & (lane < (r + 1) * HALO)
                    if c == 0:
                        shift = r * HALO % LANES
                        lo = jnp.where(mine, pltpu.roll(slabs[r], shift, 1) if shift else slabs[r], lo)
                    if c == cols // LANES - 1:
                        shift = (r + 1) * HALO % LANES
                        hi = jnp.where(mine, pltpu.roll(slabs[r], shift, 1) if shift else slabs[r], hi)
            left[a, part] = jnp.where(col_odd, hi, lo)
            right[a, part] = jnp.where(col_odd, lo, hi)


def back(x, axis):
    return pltpu.roll(x, 1, axis)


def ahead(x, axis):
    return pltpu.roll(x, x.shape[axis] - 1, axis)


def main_kernel(flags, own_odd, own_even, rows_odd, rows_even, strip_odd, strip_even, corner_odd, corner_even,
                signs, picks, mix, precond_out, image_out, sketch_out,
                res, dirn, pre, kx, ky, kz, diag, image, flip, *, depth, rows, cols, samples):
    width = cols + LANES
    half = depth // 2
    span = rows + 2 * HALO
    parts = (slice(0, half), slice(half, depth))
    odd, col_odd = flags[0] == 1, flags[1] == 1
    top, bottom, left, right = (flags[i].astype(jnp.float32) for i in range(2, 6))
    middle = (highest + lowest) / 2.0
    spread = (highest - lowest) / 2.0
    lane = lax.broadcasted_iota(jnp.int32, (half, LANES), 1)
    tail = (lane < HALO, lane >= LANES - HALO)

    def side_lanes(lo, hi, at):
        shift_hi = (LANES - at * HALO) % LANES
        shift_lo = (2 * LANES - HALO - at * HALO) % LANES
        hi = pltpu.roll(hi, shift_hi, 1) if shift_hi else hi
        lo = pltpu.roll(lo, shift_lo, 1) if shift_lo else lo
        return jnp.where(tail[0], hi, jnp.where(tail[1], lo, 0.0))

    def slabs_of(a):
        def ordered(pick):
            o, e = pick(0), pick(1)
            return jnp.where(col_odd, e, o), jnp.where(col_odd, o, e)

        own = [ordered(lambda i, t=t: (strip_odd, strip_even)[i][a, parts[t]]) for t in range(2)]
        far_odd = [ordered(lambda i, t=t: corner_odd[i, a, parts[t]]) for t in range(2)]
        far_even = [ordered(lambda i, t=t: corner_even[i, a, parts[t]]) for t in range(2)]
        above = [[jnp.where(odd, e, o) for o, e in zip(far_odd[t], far_even[t])] for t in range(2)]
        below = [[jnp.where(odd, o, e) for o, e in zip(far_odd[t], far_even[t])] for t in range(2)]
        for j in range(span):
            if j < HALO:
                slab = [jnp.where(odd, rows_even[a, j, p], rows_odd[a, j, p]) for p in parts]
                sides, at = above, rows - HALO + j
            elif j < HALO + rows:
                at = (j - HALO) % (rows - HALO)
                lower = j - HALO >= rows - HALO
                mine = (own_even, own_odd) if lower else (own_odd, own_even)
                slab = [jnp.where(odd, mine[1][a, at, p], mine[0][a, at, p]) for p in parts]
                sides, at = own, j - HALO
            else:
                at = j - HALO - rows
                slab = [jnp.where(odd, rows_odd[a, at, p], rows_even[a, at, p]) for p in parts]
                sides = below
            yield j, [jnp.concatenate([slab[t], side_lanes(*sides[t], at)], axis=1) for t in range(2)]

    for j, slab in slabs_of(0):
        for t in range(2):
            if HALO <= j < HALO + rows:
                image[j - HALO, parts[t]] = slab[t][:, :cols]
            first = slab[t] * (1.0 / middle)
            res[j, parts[t]] = slab[t]
            dirn[j, parts[t]] = first
            pre[j, parts[t]] = first[:, :cols]

    deep = lax.broadcasted_iota(jnp.int32, (half, width), 0)
    wide = lax.broadcasted_iota(jnp.int32, (half, width), 1)

    def flag(mask):
        return jnp.where(mask, 1.0, 0.0)

    sides = left * flag(wide == 0) + right * flag(wide == cols - 1)
    ends = [sides + flag(deep == 0), sides + flag(deep == half - 1)]
    x_inner = 1.0 - right * flag(wide == cols - 1) - left * flag(wide == width - 1)
    z_inner = flag(deep < half - 1)
    last = None
    for j, slab in slabs_of(1):
        halves = [0.5 * v for v in slab]
        if last is not None:
            for t in range(2):
                open_face = 1.0 - (top if j == HALO else bottom) if j in (HALO, HALO + rows) else None
                face = last[t] + halves[t]
                ky[j - 1, parts[t]] = face if open_face is None else face * open_face
        if 0 < j < span - 1:
            kz[j, parts[0]] = halves[0] + halves[1]
            kz[j, parts[1]] = (halves[1] + ahead(halves[0], 0)) * z_inner
            for t in range(2):
                kx[j, parts[t]] = (halves[t] + ahead(halves[t], 1)) * x_inner
                edge = ends[t]
                if j == HALO:
                    edge = edge + top
                if j == HALO + rows - 1:
                    edge = edge + bottom
                diag[j, parts[t]] = reaction + halves[t] * edge
        last = halves

    def sweep(low, high, emit):
        def body(j, carry):
            here, turned, flux_y = carry
            nxt = [dirn[j + 1, p] for p in parts]
            nxt_turned = [ahead(v, 1) for v in nxt]
            flux = [ky[j, parts[t]] * (here[t] - nxt[t]) for t in range(2)]
            flux_x = [kx[j, parts[t]] * (here[t] - turned[t]) for t in range(2)]
            flux_z0 = kz[j, parts[0]] * (here[0] - here[1])
            flux_z1 = kz[j, parts[1]] * (here[1] - ahead(here[0], 0))
            along_z = (flux_z0 - back(flux_z1, 0), flux_z1 - flux_z0)
            for t in range(2):
                applied = (diag[j, parts[t]] * here[t] + (flux[t] - flux_y[t])) + along_z[t]
                applied = applied + (flux_x[t] - back(flux_x[t], 1))
                emit(j, t, here[t], applied)
            return nxt, nxt_turned, flux

        before = [dirn[low - 1, p] for p in parts]
        here = [dirn[low, p] for p in parts]
        first_flux = [ky[low - 1, parts[t]] * (before[t] - here[t]) for t in range(2)]
        lax.fori_loop(low, high, body, (here, [ahead(v, 1) for v in here], first_flux))

    sig_ratio = middle / spread
    rho_now = 1.0 / sig_ratio
    for step in range(1, SWEEPS):
        rho_next = 1.0 / (2.0 * sig_ratio - rho_now)
        keep, gain = rho_next * rho_now, 2.0 * rho_next / spread
        rho_now = rho_next

        def emit(j, t, here, applied):
            left_over = res[j, parts[t]] - applied
            res[j, parts[t]] = left_over
            fresh = keep * here + gain * left_over
            dirn[j, parts[t]] = fresh
            pre[j, parts[t]] = pre[j, parts[t]] + fresh[:, :cols]

        sweep(step, span - step, emit)

    def finish(j, t, here, applied):
        row = j - HALO
        image[row, parts[t]] = image[row, parts[t]] - (res[j, parts[t], :cols] - applied[:, :cols])

    sweep(HALO, HALO + rows, finish)
    for c in range(cols // LANES):
        part = slice(c * LANES, (c + 1) * LANES)
        for r in range(0, rows, half):
            sign = signs[r : r + half, part].astype(jnp.float32)
            for t in range(2):
                kept = turn([pre[HALO + r + i, parts[t], part] for i in range(half)])
                made = turn([image[r + i, parts[t], part] for i in range(half)])
                for s in range(half):
                    cell = 2 * s + t
                    precond_out[cell, r : r + half, part] = kept[s]
                    image_out[cell, r : r + half, part] = made[s]
                    flip[cell * rows + r : cell * rows + r + half, part] = made[s] * sign
    col_ids = lax.broadcasted_iota(jnp.int32, (samples, cols), 1)
    chosen = (picks[...] == col_ids).astype(jnp.float32)
    picked = lax.dot_general(chosen, flip[...], (((1,), (1,)), ((), ())),
                             precision=lax.Precision.HIGHEST, preferred_element_type=jnp.float32)
    sketch_out[...] = lax.dot_general(picked, mix[...], (((1,), (0,)), ((), ())),
                                      precision=lax.Precision.HIGHEST, preferred_element_type=jnp.float32)


def per_device(basis_vec, conductivity, sign_vals, sample_cols):
    depth, rows, cols = basis_vec.shape
    samples = sample_cols.shape[0]
    gx_size, gy_size = lax.axis_size("gx"), lax.axis_size("gy")
    gx_index, gy_index = lax.axis_index("gx"), lax.axis_index("gy")
    flags = jnp.stack([
        gx_index & 1, gy_index & 1, gx_index == 0, gx_index == gx_size - 1, gy_index == 0, gy_index == gy_size - 1,
    ]).astype(jnp.int32)
    smem = pl.BlockSpec(memory_space=pltpu.SMEM)
    vmem = pl.BlockSpec(memory_space=pltpu.VMEM)
    sizes = dict(depth=depth, rows=rows, cols=cols)
    f32 = jnp.float32
    row_msg = jax.ShapeDtypeStruct((2, HALO, depth, cols), f32)
    strip_msg = jax.ShapeDtypeStruct((2, depth, LANES), f32)
    to_odd, to_even, strip_to_odd, strip_to_even = pl.pallas_call(
        lambda *refs: pack_kernel(*refs, **sizes),
        in_specs=[smem, vmem, vmem],
        out_specs=[vmem] * 4,
        out_shape=[row_msg, row_msg, strip_msg, strip_msg],
        compiler_params=pltpu.CompilerParams(vmem_limit_bytes=8 << 20),
        name="pack",
    )(flags, basis_vec, conductivity)
    with jax.named_scope("rows_odd"):
        rows_odd = exchange(to_odd, odd_pair, same)
    with jax.named_scope("strip_odd"):
        strip_odd = exchange(strip_to_odd, same, odd_pair)
    with jax.named_scope("strip_even"):
        strip_even = exchange(strip_to_even, same, even_pair)
    with jax.named_scope("rows_even"):
        rows_even = exchange(to_even, even_pair, same)
    strips = jnp.stack([strip_odd, strip_even])
    with jax.named_scope("corner_odd"):
        corner_odd = exchange(strips, odd_pair, same)
    with jax.named_scope("corner_even"):
        corner_even = exchange(strips, even_pair, same)
    mix = jnp.asarray(hartley_mix(depth, rows, 1.0 / np.sqrt(gx_size)))
    span, width = rows + 2 * HALO, cols + LANES
    precond, image, current = pl.pallas_call(
        lambda *refs: main_kernel(*refs, samples=samples, **sizes),
        in_specs=[smem] + [vmem] * 11,
        out_specs=[vmem] * 3,
        out_shape=[jax.ShapeDtypeStruct((depth, rows, cols), f32)] * 2
        + [jax.ShapeDtypeStruct((samples, depth * rows), f32)],
        scratch_shapes=[pltpu.VMEM((span, depth, width), f32)] * 2
        + [pltpu.VMEM((span, depth, cols), f32)]
        + [pltpu.VMEM((span, depth, width), f32)] * 4
        + [
            pltpu.VMEM((rows, depth, cols), f32),
            pltpu.VMEM((depth * rows, cols), f32),
        ],
        compiler_params=pltpu.CompilerParams(vmem_limit_bytes=24 << 20),
        name="solve",
    )(flags, to_odd, to_even, rows_odd, rows_even, strip_odd, strip_even, corner_odd, corner_even,
      sign_vals, sample_cols.reshape(samples, 1), mix)
    gx_bits = gx_size.bit_length() - 1
    for group in [[0]] + bit_groups(list(range(1, gx_bits))):
        total = walsh_sign(gx_index, 0, group) * current
        for mask in masks_of(group)[1:]:
            total = total + walsh_sign(gx_index, mask, group) * swap(current, "gx", mask)
        current = total
    for group in bit_groups(list(range(gy_size.bit_length() - 1))):
        current = current + sum(swap(current, "gy", mask) for mask in masks_of(group)[1:])
    return precond, image, current.T.reshape(depth, rows, samples)


def solution(mesh):
    in_specs = (P(None, "gx", "gy"), P(None, "gx", "gy"), P("gx", "gy"), P("gy"))
    out_specs = (P(None, "gx", "gy"), P(None, "gx", "gy"), P(None, "gx", None))
    return jax.shard_map(
        per_device, mesh=mesh, in_specs=in_specs, out_specs=out_specs, check_vma=False
    )
```

```python
import jax
import jax.numpy as jnp
import numpy as np
from jax import lax
from jax.experimental import pallas as pl
from jax.experimental.pallas import tpu as pltpu
from jax.sharding import PartitionSpec as P

SWEEPS = 8
reaction = 0.5
lowest = 0.5
highest = 62.0
HALO = SWEEPS
LANES = 128
AXES = ("gx", "gy")


def even_pair(i, n):
    return i ^ 1


def odd_pair(i, n):
    j = ((i + 1) ^ 1) - 1
    return j if 0 <= j < n else None


def same(i, n):
    return i


def exchange(array, row_map, col_map):
    rows, cols = lax.axis_size("gx"), lax.axis_size("gy")
    pairs = []
    for g in range(rows):
        for y in range(cols):
            to_g, to_y = row_map(g, rows), col_map(y, cols)
            if to_g is not None and to_y is not None:
                pairs.append((g * cols + y, to_g * cols + to_y))
    return lax.ppermute(array, AXES, pairs)


def swap(array, axis, mask):
    return lax.ppermute(array, axis, [(i, i ^ mask) for i in range(lax.axis_size(axis))])


def bit_groups(bits):
    return [bits[i : i + 2] for i in range(0, len(bits), 2)]


def masks_of(group):
    masks = [0]
    for bit in group:
        masks = masks + [m | 1 << bit for m in masks]
    return masks


def walsh_sign(index, mask, group):
    parity = jnp.int32(0)
    for bit in group:
        parity = parity + (index >> bit & (index ^ mask) >> bit & 1)
    return (1 - 2 * (parity & 1)).astype(jnp.float32)


def hartley_mix(depth, rows, scale):
    angles = (np.outer(np.arange(rows), np.arange(rows)) % rows) * (2.0 * np.pi / rows)
    table = (np.cos(angles) + np.sin(angles)) / np.sqrt(rows) * scale
    return np.kron(np.eye(depth), table.T).astype(np.float32)


def turn(tiles):
    count = len(tiles)
    sub = lax.broadcasted_iota(jnp.int32, tiles[0].shape, 0)
    tiles = list(tiles)
    step = 1
    while step < count:
        low = (sub & step) == 0
        for i in range(count):
            if not i & step:
                a, b = tiles[i], tiles[i + step]
                tiles[i] = jnp.where(low, a, pltpu.roll(b, step, 0))
                tiles[i + step] = jnp.where(low, pltpu.roll(a, count - step, 0), b)
        step *= 2
    return tiles


def pack_kernel(flags, basis, cond, to_odd, to_even, left, right, *, depth, rows, cols):
    odd, col_odd = flags[0] == 1, flags[1] == 1
    half = depth // 2
    lane = lax.broadcasted_iota(jnp.int32, (half, LANES), 1)
    for a, source in enumerate((basis, cond)):
        for t in range(2):
            part = slice(t * half, (t + 1) * half)
            lo = hi = jnp.zeros((half, LANES), jnp.float32)
            for c in range(cols // LANES):
                span = slice(c * LANES, (c + 1) * LANES)
                slabs = []
                for r in range(0, rows, half):
                    slabs += turn([source[2 * s + t, r : r + half, span] for s in range(half)])
                for r in range(HALO):
                    first, last = slabs[r], slabs[rows - HALO + r]
                    to_odd[a, r, part, span] = jnp.where(odd, last, first)
                    to_even[a, r, part, span] = jnp.where(odd, first, last)
                for r in range(rows):
                    mine = (lane >= r * HALO) & (lane < (r + 1) * HALO)
                    if c == 0:
                        shift = r * HALO % LANES
                        lo = jnp.where(mine, pltpu.roll(slabs[r], shift, 1) if shift else slabs[r], lo)
                    if c == cols // LANES - 1:
                        shift = (r + 1) * HALO % LANES
                        hi = jnp.where(mine, pltpu.roll(slabs[r], shift, 1) if shift else slabs[r], hi)
            left[a, part] = jnp.where(col_odd, hi, lo)
            right[a, part] = jnp.where(col_odd, lo, hi)


def back(x, axis):
    return pltpu.roll(x, 1, axis)


def ahead(x, axis):
    return pltpu.roll(x, x.shape[axis] - 1, axis)


def main_kernel(flags, own_odd, own_even, rows_odd, rows_even, strip_odd, strip_even, corner_odd, corner_even,
                signs, picks, mix, precond_out, image_out, sketch_out,
                res, dirn, across, pre, kx, ky, kz, diag, image, flip, *, depth, rows, cols, samples):
    width = cols + LANES
    half = depth // 2
    span = rows + 2 * HALO
    parts = (slice(0, half), slice(half, depth))
    odd, col_odd = flags[0] == 1, flags[1] == 1
    top, bottom, left, right = (flags[i].astype(jnp.float32) for i in range(2, 6))
    middle = (highest + lowest) / 2.0
    spread = (highest - lowest) / 2.0
    lane = lax.broadcasted_iota(jnp.int32, (half, LANES), 1)
    tail = (lane < HALO, lane >= LANES - HALO)

    def side_lanes(lo, hi, at):
        shift_hi = (LANES - at * HALO) % LANES
        shift_lo = (2 * LANES - HALO - at * HALO) % LANES
        hi = pltpu.roll(hi, shift_hi, 1) if shift_hi else hi
        lo = pltpu.roll(lo, shift_lo, 1) if shift_lo else lo
        return jnp.where(tail[0], hi, jnp.where(tail[1], lo, 0.0))

    def slabs_of(a):
        def ordered(pick):
            o, e = pick(0), pick(1)
            return jnp.where(col_odd, e, o), jnp.where(col_odd, o, e)

        own = [ordered(lambda i, t=t: (strip_odd, strip_even)[i][a, parts[t]]) for t in range(2)]
        far_odd = [ordered(lambda i, t=t: corner_odd[i, a, parts[t]]) for t in range(2)]
        far_even = [ordered(lambda i, t=t: corner_even[i, a, parts[t]]) for t in range(2)]
        above = [[jnp.where(odd, e, o) for o, e in zip(far_odd[t], far_even[t])] for t in range(2)]
        below = [[jnp.where(odd, o, e) for o, e in zip(far_odd[t], far_even[t])] for t in range(2)]
        for j in range(span):
            if j < HALO:
                slab = [jnp.where(odd, rows_even[a, j, p], rows_odd[a, j, p]) for p in parts]
                sides, at = above, rows - HALO + j
            elif j < HALO + rows:
                at = (j - HALO) % (rows - HALO)
                lower = j - HALO >= rows - HALO
                mine = (own_even, own_odd) if lower else (own_odd, own_even)
                slab = [jnp.where(odd, mine[1][a, at, p], mine[0][a, at, p]) for p in parts]
                sides, at = own, j - HALO
            else:
                at = j - HALO - rows
                slab = [jnp.where(odd, rows_odd[a, at, p], rows_even[a, at, p]) for p in parts]
                sides = below
            yield j, [jnp.concatenate([slab[t], side_lanes(*sides[t], at)], axis=1) for t in range(2)]

    for j, slab in slabs_of(0):
        for t in range(2):
            if HALO <= j < HALO + rows:
                image[j - HALO, parts[t]] = slab[t][:, :cols]
            first = slab[t] * (1.0 / middle)
            res[j, parts[t]] = slab[t]
            dirn[j, parts[t]] = first
            pre[j, parts[t]] = first[:, :cols]

    deep = lax.broadcasted_iota(jnp.int32, (half, width), 0)
    wide = lax.broadcasted_iota(jnp.int32, (half, width), 1)

    def flag(mask):
        return jnp.where(mask, 1.0, 0.0)

    sides = left * flag(wide == 0) + right * flag(wide == cols - 1)
    ends = [sides + flag(deep == 0), sides + flag(deep == half - 1)]
    x_inner = 1.0 - right * flag(wide == cols - 1) - left * flag(wide == width - 1)
    z_inner = flag(deep < half - 1)
    last = None
    for j, slab in slabs_of(1):
        halves = [0.5 * v for v in slab]
        if last is not None:
            for t in range(2):
                open_face = 1.0 - (top if j == HALO else bottom) if j in (HALO, HALO + rows) else None
                face = last[t] + halves[t]
                ky[j - 1, parts[t]] = face if open_face is None else face * open_face
        if 0 < j < span - 1:
            kz[j, parts[0]] = halves[0] + halves[1]
            kz[j, parts[1]] = (halves[1] + ahead(halves[0], 0)) * z_inner
            for t in range(2):
                kx[j, parts[t]] = (halves[t] + ahead(halves[t], 1)) * x_inner
                edge = ends[t]
                if j == HALO:
                    edge = edge + top
                if j == HALO + rows - 1:
                    edge = edge + bottom
                diag[j, parts[t]] = reaction + halves[t] * edge
        last = halves

    def sweep(low, high, emit):
        for j in range(low, high):
            for t in range(2):
                here = dirn[j, parts[t]]
                across[j, parts[t]] = kx[j, parts[t]] * (here - ahead(here, 1))
        here = [dirn[low, p] for p in parts]
        flux_y = [ky[low - 1, parts[t]] * (dirn[low - 1, parts[t]] - here[t]) for t in range(2)]
        for j in range(low, high):
            nxt = [dirn[j + 1, p] for p in parts]
            flux = [ky[j, parts[t]] * (here[t] - nxt[t]) for t in range(2)]
            flux_z0 = kz[j, parts[0]] * (here[0] - here[1])
            flux_z1 = kz[j, parts[1]] * (here[1] - ahead(here[0], 0))
            along_z = (flux_z0 - back(flux_z1, 0), flux_z1 - flux_z0)
            for t in range(2):
                flux_x = across[j, parts[t]]
                applied = (diag[j, parts[t]] * here[t] + (flux[t] - flux_y[t])) + along_z[t]
                emit(j, t, here[t], applied + (flux_x - back(flux_x, 1)))
            here, flux_y = nxt, flux

    sig_ratio = middle / spread
    rho_now = 1.0 / sig_ratio
    for step in range(1, SWEEPS):
        rho_next = 1.0 / (2.0 * sig_ratio - rho_now)
        keep, gain = rho_next * rho_now, 2.0 * rho_next / spread
        rho_now = rho_next

        def emit(j, t, here, applied):
            left_over = res[j, parts[t]] - applied
            res[j, parts[t]] = left_over
            fresh = keep * here + gain * left_over
            dirn[j, parts[t]] = fresh
            pre[j, parts[t]] = pre[j, parts[t]] + fresh[:, :cols]

        sweep(step, span - step, emit)

    def finish(j, t, here, applied):
        row = j - HALO
        image[row, parts[t]] = image[row, parts[t]] - (res[j, parts[t], :cols] - applied[:, :cols])

    sweep(HALO, HALO + rows, finish)
    for c in range(cols // LANES):
        part = slice(c * LANES, (c + 1) * LANES)
        for r in range(0, rows, half):
            sign = signs[r : r + half, part].astype(jnp.float32)
            for t in range(2):
                kept = turn([pre[HALO + r + i, parts[t], part] for i in range(half)])
                made = turn([image[r + i, parts[t], part] for i in range(half)])
                for s in range(half):
                    cell = 2 * s + t
                    precond_out[cell, r : r + half, part] = kept[s]
                    image_out[cell, r : r + half, part] = made[s]
                    flip[cell * rows + r : cell * rows + r + half, part] = made[s] * sign
    col_ids = lax.broadcasted_iota(jnp.int32, (samples, cols), 1)
    chosen = (picks[...] == col_ids).astype(jnp.float32)
    picked = lax.dot_general(chosen, flip[...], (((1,), (1,)), ((), ())),
                             precision=lax.Precision.HIGHEST, preferred_element_type=jnp.float32)
    sketch_out[...] = lax.dot_general(picked, mix[...], (((1,), (0,)), ((), ())),
                                      precision=lax.Precision.HIGHEST, preferred_element_type=jnp.float32)


def per_device(basis_vec, conductivity, sign_vals, sample_cols):
    depth, rows, cols = basis_vec.shape
    samples = sample_cols.shape[0]
    gx_size, gy_size = lax.axis_size("gx"), lax.axis_size("gy")
    gx_index, gy_index = lax.axis_index("gx"), lax.axis_index("gy")
    flags = jnp.stack([
        gx_index & 1, gy_index & 1, gx_index == 0, gx_index == gx_size - 1, gy_index == 0, gy_index == gy_size - 1,
    ]).astype(jnp.int32)
    smem = pl.BlockSpec(memory_space=pltpu.SMEM)
    vmem = pl.BlockSpec(memory_space=pltpu.VMEM)
    sizes = dict(depth=depth, rows=rows, cols=cols)
    f32 = jnp.float32
    row_msg = jax.ShapeDtypeStruct((2, HALO, depth, cols), f32)
    strip_msg = jax.ShapeDtypeStruct((2, depth, LANES), f32)
    to_odd, to_even, strip_to_odd, strip_to_even = pl.pallas_call(
        lambda *refs: pack_kernel(*refs, **sizes),
        in_specs=[smem, vmem, vmem],
        out_specs=[vmem] * 4,
        out_shape=[row_msg, row_msg, strip_msg, strip_msg],
        compiler_params=pltpu.CompilerParams(vmem_limit_bytes=8 << 20),
        name="pack",
    )(flags, basis_vec, conductivity)
    with jax.named_scope("rows_odd"):
        rows_odd = exchange(to_odd, odd_pair, same)
    with jax.named_scope("strip_odd"):
        strip_odd = exchange(strip_to_odd, same, odd_pair)
    with jax.named_scope("strip_even"):
        strip_even = exchange(strip_to_even, same, even_pair)
    with jax.named_scope("rows_even"):
        rows_even = exchange(to_even, even_pair, same)
    strips = jnp.stack([strip_odd, strip_even])
    with jax.named_scope("corner_odd"):
        corner_odd = exchange(strips, odd_pair, same)
    with jax.named_scope("corner_even"):
        corner_even = exchange(strips, even_pair, same)
    mix = jnp.asarray(hartley_mix(depth, rows, 1.0 / np.sqrt(gx_size)))
    span, width = rows + 2 * HALO, cols + LANES
    precond, image, current = pl.pallas_call(
        lambda *refs: main_kernel(*refs, samples=samples, **sizes),
        in_specs=[smem] + [vmem] * 11,
        out_specs=[vmem] * 3,
        out_shape=[jax.ShapeDtypeStruct((depth, rows, cols), f32)] * 2
        + [jax.ShapeDtypeStruct((samples, depth * rows), f32)],
        scratch_shapes=[pltpu.VMEM((span, depth, width), f32)] * 3
        + [pltpu.VMEM((span, depth, cols), f32)]
        + [pltpu.VMEM((span, depth, width), f32)] * 4
        + [
            pltpu.VMEM((rows, depth, cols), f32),
            pltpu.VMEM((depth * rows, cols), f32),
        ],
        compiler_params=pltpu.CompilerParams(vmem_limit_bytes=24 << 20),
        name="solve",
    )(flags, to_odd, to_even, rows_odd, rows_even, strip_odd, strip_even, corner_odd, corner_even,
      sign_vals, sample_cols.reshape(samples, 1), mix)
    gx_bits = gx_size.bit_length() - 1
    for group in [[0]] + bit_groups(list(range(1, gx_bits))):
        total = walsh_sign(gx_index, 0, group) * current
        for mask in masks_of(group)[1:]:
            total = total + walsh_sign(gx_index, mask, group) * swap(current, "gx", mask)
        current = total
    for group in bit_groups(list(range(gy_size.bit_length() - 1))):
        current = current + sum(swap(current, "gy", mask) for mask in masks_of(group)[1:])
    return precond, image, current.T.reshape(depth, rows, samples)


def solution(mesh):
    in_specs = (P(None, "gx", "gy"), P(None, "gx", "gy"), P("gx", "gy"), P("gy"))
    out_specs = (P(None, "gx", "gy"), P(None, "gx", "gy"), P(None, "gx", None))
    return jax.shard_map(
        per_device, mesh=mesh, in_specs=in_specs, out_specs=out_specs, check_vma=False
    )
```

```python
import jax
import jax.numpy as jnp
import numpy as np
from jax import lax
from jax.experimental import pallas as pl
from jax.experimental.pallas import tpu as pltpu
from jax.sharding import PartitionSpec as P


SWEEPS = 8
reaction = 0.5
lowest = 0.5
highest = 62.0
HALO = SWEEPS
LANES = 128
AXES = ("gx", "gy")


def even_pair(i, n):
    return i ^ 1


def odd_pair(i, n):
    j = ((i + 1) ^ 1) - 1
    return j if 0 <= j < n else None


def same(i, n):
    return i


def exchange(array, row_map, col_map):
    rows, cols = lax.axis_size("gx"), lax.axis_size("gy")
    pairs = []
    for g in range(rows):
        for y in range(cols):
            to_g, to_y = row_map(g, rows), col_map(y, cols)
            if to_g is not None and to_y is not None:
                pairs.append((g * cols + y, to_g * cols + to_y))
    return lax.ppermute(array, AXES, pairs)


def swap(array, axis, mask):
    return lax.ppermute(array, axis, [(i, i ^ mask) for i in range(lax.axis_size(axis))])


def bit_groups(bits):
    return [bits[i : i + 2] for i in range(0, len(bits), 2)]


def masks_of(group):
    masks = [0]
    for bit in group:
        masks = masks + [m | 1 << bit for m in masks]
    return masks


def walsh_sign(index, mask, group):
    parity = jnp.int32(0)
    for bit in group:
        parity = parity + (index >> bit & (index ^ mask) >> bit & 1)
    return (1 - 2 * (parity & 1)).astype(jnp.float32)


def hartley_mix(depth, rows, scale):
    angles = (np.outer(np.arange(rows), np.arange(rows)) % rows) * (2.0 * np.pi / rows)
    table = (np.cos(angles) + np.sin(angles)) / np.sqrt(rows) * scale
    slots = np.arange(depth)
    placed = np.eye(depth)[2 * (slots % (depth // 2)) + slots // (depth // 2)]
    return np.einsum("jk,se->ksej", table, placed).reshape(rows * depth, depth * rows).astype(np.float32)


def turn(tiles):
    count = len(tiles)
    sub = lax.broadcasted_iota(jnp.int32, tiles[0].shape, 0)
    tiles = list(tiles)
    step = 1
    while step < count:
        low = (sub & step) == 0
        for i in range(count):
            if not i & step:
                a, b = tiles[i], tiles[i + step]
                tiles[i] = jnp.where(low, a, pltpu.roll(b, step, 0))
                tiles[i + step] = jnp.where(low, pltpu.roll(a, count - step, 0), b)
        step *= 2
    return tiles


def back(x, axis):
    return pltpu.roll(x, 1, axis)


def ahead(x, axis):
    return pltpu.roll(x, x.shape[axis] - 1, axis)


def flag(mask):
    return jnp.where(mask, 1.0, 0.0)


def move(x, shift):
    return pltpu.roll(x, shift % LANES, 1) if shift % LANES else x


def pack_kernel(flags, basis, cond, to_odd, to_even, left, right, held, sems, *, depth, rows, cols):
    odd, col_odd = flags[0] == 1, flags[1] == 1
    half = depth // 2
    lane = lax.broadcasted_iota(jnp.int32, (half, LANES), 1)
    tiles = cols // LANES

    def load(a, c):
        source = (basis, cond)[a].at[:, :, pl.ds(c * LANES, LANES)]
        return pltpu.make_async_copy(source, held.at[a, c], sems.at[a, c])

    for a in range(2):
        for c in range(tiles):
            load(a, c).start()
    for a in range(2):
        lo = [jnp.zeros((half, LANES), jnp.float32)] * 2
        hi = [jnp.zeros((half, LANES), jnp.float32)] * 2
        for c in range(tiles):
            load(a, c).wait()
            span = slice(c * LANES, (c + 1) * LANES)
            for t in range(2):
                part = slice(t * half, (t + 1) * half)
                slabs = []
                for r in range(0, rows, half):
                    slabs += turn([held[a, c, 2 * s + t, r : r + half, :] for s in range(half)])
                slabs = [jnp.where(odd, slabs[rows - 1 - i], slabs[i]) for i in range(rows)]
                for i in range(HALO):
                    to_odd[a * HALO + i, part, span] = slabs[i]
                    to_even[a * HALO + i, part, span] = slabs[rows - HALO + i]
                for i in range(rows):
                    mine = (lane >= i * HALO) & (lane < (i + 1) * HALO)
                    if c == 0:
                        lo[t] = jnp.where(mine, move(slabs[i], i * HALO), lo[t])
                    if c == tiles - 1:
                        hi[t] = jnp.where(mine, move(slabs[i], (i + 1) * HALO), hi[t])
        for t in range(2):
            part = slice(t * half, (t + 1) * half)
            left[a, part] = jnp.where(col_odd, hi[t], lo[t])
            right[a, part] = jnp.where(col_odd, lo[t], hi[t])
    for target in (to_odd, to_even):
        target[2 * HALO] = jnp.zeros((depth, cols), jnp.float32)


def corner_kernel(to_odd, to_even, strip_odd, strip_even, odd_out, even_out, *, depth):
    lane = lax.broadcasted_iota(jnp.int32, (depth, LANES), 1)
    first = lane < LANES // 2
    for a in range(2):
        span = slice(a * LANES, (a + 1) * LANES)
        even, odd = strip_even[a], strip_odd[a]
        odd_out[2 * HALO, :, span] = jnp.where(first, even, move(odd, LANES // 2))
        even_out[2 * HALO, :, span] = jnp.where(first, move(even, LANES // 2), odd)


class Field:
    def __init__(self):
        self.where = {}

    def put(self, first, ref, count):
        for i in range(count):
            self.where[first + i] = (ref, i)

    def get(self, j, part):
        ref, i = self.where[j]
        return ref[i, part]

    def set(self, j, part, value):
        ref, i = self.where[j]
        ref[i, part] = value


class Shape:
    def __init__(self, flags, depth, rows, cols):
        self.depth, self.rows, self.cols = depth, rows, cols
        self.half, self.width, self.span = depth // 2, cols + LANES, rows + 2 * HALO
        self.parts = (slice(0, self.half), slice(self.half, depth))
        self.odd, self.col_odd = flags[0] == 1, flags[1] == 1
        self.edge, self.left, self.right = (flags[i].astype(jnp.float32) for i in range(2, 5))
        self.lane = lax.broadcasted_iota(jnp.int32, (self.half, LANES), 1)
        deep = lax.broadcasted_iota(jnp.int32, (self.half, self.width), 0)
        wide = lax.broadcasted_iota(jnp.int32, (self.half, self.width), 1)
        sides = self.left * flag(wide == 0) + self.right * flag(wide == cols - 1)
        self.ends = [sides + flag(deep == 0), sides + flag(deep == self.half - 1)]
        self.x_inner = 1.0 - self.right * flag(wide == cols - 1) - self.left * flag(wide == self.width - 1)
        self.z_inner = flag(deep < self.half - 1)

    def ordered(self, odd, even):
        return jnp.where(self.col_odd, even, odd), jnp.where(self.col_odd, odd, even)

    def side(self, lo, hi, at):
        hi, lo = move(hi, -at * HALO), move(lo, -HALO - at * HALO)
        return jnp.where(self.lane < HALO, hi, jnp.where(self.lane >= LANES - HALO, lo, 0.0))

    def corner(self, message, a, t):
        both = message[2 * HALO, self.parts[t], a * LANES : (a + 1) * LANES]
        return self.ordered(move(both, LANES // 2), both)

    def slab(self, message, a, i, strips, at):
        return [
            jnp.concatenate([message[a * HALO + i, self.parts[t]], self.side(*strips[t], at)], axis=1)
            for t in range(2)
        ]

    def coefficients(self, j, halves, f, own_edge):
        f["kz"].set(j, self.parts[0], halves[0] + halves[1])
        f["kz"].set(j, self.parts[1], (halves[1] + ahead(halves[0], 0)) * self.z_inner)
        for t in range(2):
            f["kx"].set(j, self.parts[t], (halves[t] + ahead(halves[t], 1)) * self.x_inner)
            ends = self.ends[t] + self.edge if own_edge else self.ends[t]
            f["diag"].set(j, self.parts[t], reaction + halves[t] * ends)


def steps():
    middle = (highest + lowest) / 2.0
    spread = (highest - lowest) / 2.0
    sig_ratio = middle / spread
    rho_now = 1.0 / sig_ratio
    for step in range(1, SWEEPS):
        rho_next = 1.0 / (2.0 * sig_ratio - rho_now)
        yield step, rho_next * rho_now, 2.0 * rho_next / spread
        rho_now = rho_next


def apply_rows(sh, f, across, low, high, flux_low, flux_high, emit):
    parts = sh.parts
    for j in range(low, high):
        for t in range(2):
            here = f["dirn"].get(j, parts[t])
            across[j - low, parts[t]] = f["kx"].get(j, parts[t]) * (here - ahead(here, 1))
    here = [f["dirn"].get(low, p) for p in parts]
    flux_y = [f["ky"].get(low - 1, parts[t]) * (f["dirn"].get(low - 1, parts[t]) - here[t]) for t in range(2)]
    if flux_low is not None:
        for t in range(2):
            flux_low(t, flux_y[t])
    for j in range(low, high):
        if j == high - 1 and flux_high is not None:
            nxt, flux = None, [flux_high(t) for t in range(2)]
        else:
            nxt = [f["dirn"].get(j + 1, p) for p in parts]
            flux = [f["ky"].get(j, parts[t]) * (here[t] - nxt[t]) for t in range(2)]
        flux_z0 = f["kz"].get(j, parts[0]) * (here[0] - here[1])
        flux_z1 = f["kz"].get(j, parts[1]) * (here[1] - ahead(here[0], 0))
        along_z = (flux_z0 - back(flux_z1, 0), flux_z1 - flux_z0)
        for t in range(2):
            flux_x = across[j - low, parts[t]]
            applied = (f["diag"].get(j, parts[t]) * here[t] + (flux[t] - flux_y[t])) + along_z[t]
            emit(j, t, here[t], applied + (flux_x - back(flux_x, 1)))
        here, flux_y = nxt, flux


def near_kernel(flags, own_odd, own_even, rows_even, strip_odd, strip_even,
                dirn_a, res_a, pre_a, kx_a, ky_a, kz_a, diag_a, saved, edge_half, image_b, pre_b,
                dirn_b, res_b, kx_b, ky_b, kz_b, diag_b, across, *, depth, rows, cols):
    sh = Shape(flags, depth, rows, cols)
    parts = sh.parts
    mid = 2 * HALO
    f = {name: Field() for name in ("dirn", "res", "pre", "kx", "ky", "kz", "diag")}
    lows = dict(dirn=dirn_a, res=res_a, pre=pre_a, kx=kx_a, ky=ky_a, kz=kz_a, diag=diag_a)
    highs = dict(dirn=dirn_b, res=res_b, pre=pre_b, kx=kx_b, ky=ky_b, kz=kz_b, diag=diag_b)
    for name, field in f.items():
        field.put(HALO, lows[name], HALO)
    for name, ref in highs.items():
        f[name].put(mid, ref, sh.span - mid)
    f["pre"].put(mid, pre_b, HALO + rows - mid)

    def slabs_of(a):
        own = [sh.ordered(strip_odd[a, p], strip_even[a, p]) for p in parts]
        far = [sh.corner(rows_even, a, t) for t in range(2)]
        for i in range(rows):
            message = own_odd if i < HALO else own_even
            yield HALO + i, sh.slab(message, a, i % HALO if i < HALO else i - (rows - HALO), own, i)
        for k in range(HALO):
            yield HALO + rows + k, sh.slab(rows_even, a, HALO - 1 - k, far, HALO - 1 - k)

    middle = (highest + lowest) / 2.0
    for j, slab in slabs_of(0):
        for t in range(2):
            first = slab[t] * (1.0 / middle)
            f["res"].set(j, parts[t], slab[t])
            f["dirn"].set(j, parts[t], first)
            if j < HALO + rows:
                f["pre"].set(j, parts[t], first[:, :cols])
    last = None
    for j, slab in slabs_of(1):
        halves = [0.5 * v for v in slab]
        if last is not None:
            for t in range(2):
                f["ky"].set(j - 1, parts[t], last[t] + halves[t])
        else:
            for t in range(2):
                edge_half[parts[t]] = halves[t]
        if j < sh.span - 1:
            sh.coefficients(j, halves, f, j == HALO)
        last = halves

    for step, keep, gain in steps():

        def emit(j, t, here, applied):
            left_over = f["res"].get(j, parts[t]) - applied
            f["res"].set(j, parts[t], left_over)
            fresh = keep * here + gain * left_over
            f["dirn"].set(j, parts[t], fresh)
            if j < HALO + rows:
                f["pre"].set(j, parts[t], f["pre"].get(j, parts[t]) + fresh[:, :cols])

        def save(t, flux, step=step):
            saved[step - 1, parts[t]] = flux

        apply_rows(sh, f, across, HALO + step, sh.span - step, save, None, emit)

    def finish(j, t, here, applied):
        start = own_even[j - mid, parts[t]]
        image_b[j - mid, parts[t]] = start - (f["res"].get(j, parts[t])[:, :cols] - applied[:, :cols])

    def save_last(t, flux):
        saved[SWEEPS - 1, parts[t]] = flux

    apply_rows(sh, f, across, HALO + SWEEPS, HALO + rows, save_last, None, finish)


def split(x):
    high = x.astype(jnp.bfloat16)
    return high, (x - high.astype(jnp.float32)).astype(jnp.bfloat16)


def far_kernel(flags, rows_odd, own_odd, dirn_a, res_a, pre_a, kx_a, ky_a, kz_a, diag_a, saved, edge_half, image_b, pre_b,
               signs, picks, mix, image, pre, sketch_out,
               dirn, res, kx, ky, kz, diag, across, flip_high, flip_low, *, depth, rows, cols, samples):
    sh = Shape(flags, depth, rows, cols)
    parts = sh.parts
    f = {name: Field() for name in ("dirn", "res", "pre", "kx", "ky", "kz", "diag")}
    mine = dict(dirn=dirn, res=res, kx=kx, ky=ky, kz=kz, diag=diag)
    given = dict(dirn=dirn_a, res=res_a, pre=pre_a, kx=kx_a, ky=ky_a, kz=kz_a, diag=diag_a)
    for name, field in f.items():
        if name in mine:
            field.put(0, mine[name], HALO)
        field.put(HALO, given[name], HALO)
    middle = (highest + lowest) / 2.0
    corners = [[sh.corner(rows_odd, a, t) for t in range(2)] for a in range(2)]
    last = None
    for k in reversed(range(HALO)):
        j = HALO - 1 - k
        slab = sh.slab(rows_odd, 0, k, corners[0], k)
        for t in range(2):
            f["res"].set(j, parts[t], slab[t])
            f["dirn"].set(j, parts[t], slab[t] * (1.0 / middle))
        halves = [0.5 * v for v in sh.slab(rows_odd, 1, k, corners[1], k)]
        if last is not None:
            for t in range(2):
                f["ky"].set(j - 1, parts[t], last[t] + halves[t])
        if j > 0:
            sh.coefficients(j, halves, f, False)
        last = halves
    for t in range(2):
        f["ky"].set(HALO - 1, parts[t], (last[t] + edge_half[parts[t]]) * (1.0 - sh.edge))

    def hand_over(j, t):
        if j >= HALO and t == 1:
            f["dirn"].where[j] = (dirn, j)
            f["res"].where[j] = (res, j)
            f["pre"].where[j] = (pre, j - HALO)

    for step, keep, gain in steps():

        def emit(j, t, here, applied):
            left_over = f["res"].get(j, parts[t]) - applied
            fresh = keep * here + gain * left_over
            at = parts[t]
            res[j, at] = left_over
            dirn[j, at] = fresh
            if j >= HALO:
                pre[j - HALO, at] = f["pre"].get(j, at) + fresh[:, :cols]
            hand_over(j, t)

        apply_rows(sh, f, across, step, HALO + step, None, lambda t, step=step: saved[step - 1, parts[t]], emit)

    def finish(j, t, here, applied):
        start = own_odd[j - HALO, parts[t]]
        image[j - HALO, parts[t]] = start - (f["res"].get(j, parts[t])[:, :cols] - applied[:, :cols])

    apply_rows(sh, f, across, HALO, 2 * HALO, None, lambda t: saved[SWEEPS - 1, parts[t]], finish)
    for i in range(rows):
        if i >= HALO:
            image[i] = image_b[i - HALO]
            pre[i] = pre_b[i - HALO]
        elif f["pre"].where[HALO + i][0] is not pre:
            pre[i] = pre_a[i]
    for r in range(rows):
        flipped = image[r + flags[0] * (rows - 1 - 2 * r)] * signs[r : r + 1, :].astype(jnp.float32)
        at = slice(r * depth, (r + 1) * depth)
        flip_high[at], flip_low[at] = split(flipped)

    def dot(a, b, dims):
        return lax.dot_general(a, b, (dims, ((), ())), preferred_element_type=jnp.float32)

    col_ids = lax.broadcasted_iota(jnp.int32, (samples, cols), 1)
    chosen = (picks[...] == col_ids).astype(jnp.float32).astype(jnp.bfloat16)
    picked = dot(chosen, flip_high[...], ((1,), (1,))) + dot(chosen, flip_low[...], ((1,), (1,)))
    high, low = split(picked)
    rest = dot(high, mix[1], ((1,), (0,))) + dot(low, mix[0], ((1,), (0,)))
    sketch_out[...] = dot(high, mix[0], ((1,), (0,))) + rest


def tail_kernel(flags, pre, image, precond_out, image_out, *, depth, rows, cols):
    half = depth // 2
    for c in range(cols // LANES):
        span = slice(c * LANES, (c + 1) * LANES)
        for r in range(0, rows, half):
            for t in range(2):
                part = slice(t * half, (t + 1) * half)
                for source, target in ((pre, precond_out), (image, image_out)):
                    found = [source[r + i + flags[0] * (rows - 1 - 2 * (r + i)), part, span] for i in range(half)]
                    for s, tile in enumerate(turn(found)):
                        target[2 * s + t, r : r + half, span] = tile


def whole_step(basis_vec, conductivity, sign_vals, sample_cols):
    depth, rows, cols = basis_vec.shape
    samples = sample_cols.shape[0]
    assert depth == 16 and rows == 2 * HALO and cols == 2 * LANES
    gx_size, gy_size = lax.axis_size("gx"), lax.axis_size("gy")
    gx_index, gy_index = lax.axis_index("gx"), lax.axis_index("gy")
    flags = jnp.stack([
        gx_index & 1, gy_index & 1, (gx_index == 0) | (gx_index == gx_size - 1), gy_index == 0, gy_index == gy_size - 1,
    ]).astype(jnp.int32)
    smem, vmem = pl.BlockSpec(memory_space=pltpu.SMEM), pl.BlockSpec(memory_space=pltpu.VMEM)
    f32 = jnp.float32
    sizes = dict(depth=depth, rows=rows, cols=cols)
    width, span, mid = cols + LANES, rows + 2 * HALO, 2 * HALO
    wide = lambda n: jax.ShapeDtypeStruct((n, depth, width), f32)
    slim = lambda n: jax.ShapeDtypeStruct((n, depth, cols), f32)
    wide_scratch = lambda n: pltpu.VMEM((n, depth, width), f32)
    small = lambda mib: pltpu.CompilerParams(vmem_limit_bytes=mib << 20)
    message = slim(2 * HALO + 1)
    strip = jax.ShapeDtypeStruct((2, depth, LANES), f32)
    own_odd, own_even, strip_to_odd, strip_to_even = pl.pallas_call(
        lambda *refs: pack_kernel(*refs, **sizes),
        in_specs=[smem] + [pl.BlockSpec(memory_space=pl.ANY)] * 2,
        out_specs=[vmem] * 4,
        out_shape=[message, message, strip, strip],
        scratch_shapes=[
            pltpu.VMEM((2, cols // LANES, depth, rows, LANES), f32),
            pltpu.SemaphoreType.DMA((2, cols // LANES)),
        ],
        compiler_params=small(4),
        name="pack",
    )(flags, basis_vec, conductivity)
    strip_even = exchange(strip_to_even, same, even_pair)
    strip_odd = exchange(strip_to_odd, same, odd_pair)
    own_odd, own_even = pl.pallas_call(
        lambda *refs: corner_kernel(*refs, depth=depth),
        in_specs=[vmem] * 4,
        out_specs=[vmem] * 2,
        out_shape=[message, message],
        input_output_aliases={0: 0, 1: 1},
        compiler_params=small(4),
        name="corners",
    )(own_odd, own_even, strip_odd, strip_even)
    rows_odd = exchange(own_odd, odd_pair, same)
    rows_even = exchange(own_even, even_pair, same)
    *handed, image_b, pre_b = pl.pallas_call(
        lambda *refs: near_kernel(*refs, **sizes),
        in_specs=[smem] + [vmem] * 5,
        out_specs=[vmem] * 11,
        out_shape=[wide(HALO), wide(HALO), slim(HALO), wide(HALO), wide(HALO), wide(HALO), wide(HALO), wide(SWEEPS),
                   jax.ShapeDtypeStruct((depth, width), f32), slim(rows - HALO), slim(rows - HALO)],
        scratch_shapes=[wide_scratch(span - mid)] * 6 + [wide_scratch(span - HALO)],
        compiler_params=small(16),
        name="near",
    )(flags, own_odd, own_even, rows_even, strip_odd, strip_even)
    mix = hartley_mix(depth, rows, 1.0 / np.sqrt(gx_size))
    mix_high = mix.astype(jnp.bfloat16)
    mix = jnp.asarray(np.stack([mix_high, (mix - mix_high.astype(np.float32)).astype(jnp.bfloat16)]))
    image, pre, current = pl.pallas_call(
        lambda *refs: far_kernel(*refs, samples=samples, **sizes),
        in_specs=[smem] + [vmem] * 16,
        out_specs=[vmem] * 3,
        out_shape=[slim(rows), slim(rows), jax.ShapeDtypeStruct((samples, depth * rows), f32)],
        scratch_shapes=[wide_scratch(mid)] * 2 + [wide_scratch(HALO)] * 5
        + [pltpu.VMEM((depth * rows, cols), jnp.bfloat16)] * 2,
        compiler_params=small(16),
        name="far",
    )(flags, rows_odd, own_odd, *handed, image_b, pre_b, sign_vals, sample_cols.reshape(samples, 1), mix)
    precond_out, image_out = pl.pallas_call(
        lambda *refs: tail_kernel(*refs, **sizes),
        in_specs=[smem] + [vmem] * 2,
        out_specs=[vmem] * 2,
        out_shape=[jax.ShapeDtypeStruct((depth, rows, cols), f32)] * 2,
        compiler_params=small(8),
        name="tail",
    )(flags, pre, image)
    gx_bits = gx_size.bit_length() - 1
    for group in [[0]] + bit_groups(list(range(1, gx_bits))):
        total = walsh_sign(gx_index, 0, group) * current
        for mask in masks_of(group)[1:]:
            total = total + walsh_sign(gx_index, mask, group) * swap(current, "gx", mask)
        current = total
    for group in bit_groups(list(range(gy_size.bit_length() - 1))):
        current = current + sum(swap(current, "gy", mask) for mask in masks_of(group)[1:])
    return precond_out, image_out, current.T.reshape(depth, rows, samples)


def solution(mesh):
    in_specs = (P(None, "gx", "gy"), P(None, "gx", "gy"), P("gx", "gy"), P("gy"))
    out_specs = (P(None, "gx", "gy"), P(None, "gx", "gy"), P(None, "gx", None))
    return jax.shard_map(whole_step, mesh=mesh, in_specs=in_specs, out_specs=out_specs, check_vma=False)
```

```python
import jax
import jax.numpy as jnp
import numpy as np
from jax import lax
from jax.experimental import pallas as pl
from jax.experimental.pallas import tpu as pltpu
from jax.sharding import PartitionSpec as P


SWEEPS = 8
reaction = 0.5
lowest = 0.5
highest = 62.0
HALO = SWEEPS
LANES = 128
AXES = ("gx", "gy")


def even_pair(i, n):
    return i ^ 1


def odd_pair(i, n):
    j = ((i + 1) ^ 1) - 1
    return j if 0 <= j < n else None


def same(i, n):
    return i


def exchange(array, row_map, col_map):
    rows, cols = lax.axis_size("gx"), lax.axis_size("gy")
    pairs = []
    for g in range(rows):
        for y in range(cols):
            to_g, to_y = row_map(g, rows), col_map(y, cols)
            if to_g is not None and to_y is not None:
                pairs.append((g * cols + y, to_g * cols + to_y))
    return lax.ppermute(array, AXES, pairs)


def swap(array, axis, mask):
    return lax.ppermute(array, axis, [(i, i ^ mask) for i in range(lax.axis_size(axis))])


def bit_groups(bits):
    return [bits[i : i + 2] for i in range(0, len(bits), 2)]


def masks_of(group):
    masks = [0]
    for bit in group:
        masks = masks + [m | 1 << bit for m in masks]
    return masks


def walsh_sign(index, mask, group):
    parity = jnp.int32(0)
    for bit in group:
        parity = parity + (index >> bit & (index ^ mask) >> bit & 1)
    return (1 - 2 * (parity & 1)).astype(jnp.float32)


def hartley_mix(depth, rows, scale):
    angles = (np.outer(np.arange(rows), np.arange(rows)) % rows) * (2.0 * np.pi / rows)
    table = (np.cos(angles) + np.sin(angles)) / np.sqrt(rows) * scale
    slots = np.arange(depth)
    placed = np.eye(depth)[2 * (slots % (depth // 2)) + slots // (depth // 2)]
    return np.einsum("jk,se->ksej", table, placed).reshape(rows * depth, depth * rows).astype(np.float32)


def turn(tiles):
    count = len(tiles)
    sub = lax.broadcasted_iota(jnp.int32, tiles[0].shape, 0)
    tiles = list(tiles)
    step = 1
    while step < count:
        low = (sub & step) == 0
        for i in range(count):
            if not i & step:
                a, b = tiles[i], tiles[i + step]
                tiles[i] = jnp.where(low, a, pltpu.roll(b, step, 0))
                tiles[i + step] = jnp.where(low, pltpu.roll(a, count - step, 0), b)
        step *= 2
    return tiles


def back(x, axis):
    return pltpu.roll(x, 1, axis)


def ahead(x, axis):
    return pltpu.roll(x, x.shape[axis] - 1, axis)


def flag(mask):
    return jnp.where(mask, 1.0, 0.0)


def position():
    gx, gy = lax.axis_index("gx"), lax.axis_index("gy")
    last_gx, last_gy = lax.axis_size("gx") - 1, lax.axis_size("gy") - 1
    return gx & 1, gy & 1, (gx == 0) | (gx == last_gx), gy == 0, gy == last_gy


def move(x, shift):
    return pltpu.roll(x, shift % LANES, 1) if shift % LANES else x


def pack_kernel(basis, cond, to_odd, to_even, left, right, held, sems, *, depth, rows, cols):
    flags = position()
    odd, col_odd = flags[0] == 1, flags[1] == 1
    half = depth // 2
    lane = lax.broadcasted_iota(jnp.int32, (half, LANES), 1)
    tiles = cols // LANES

    def load(a, c):
        source = (basis, cond)[a].at[:, :, pl.ds(c * LANES, LANES)]
        return pltpu.make_async_copy(source, held.at[a, c], sems.at[a, c])

    for a in range(2):
        for c in range(tiles):
            load(a, c).start()
    for a in range(2):
        lo = [jnp.zeros((half, LANES), jnp.float32)] * 2
        hi = [jnp.zeros((half, LANES), jnp.float32)] * 2
        for c in range(tiles):
            load(a, c).wait()
            span = slice(c * LANES, (c + 1) * LANES)
            for t in range(2):
                part = slice(t * half, (t + 1) * half)
                slabs = []
                for r in range(0, rows, half):
                    slabs += turn([held[a, c, 2 * s + t, r : r + half, :] for s in range(half)])
                slabs = [jnp.where(odd, slabs[rows - 1 - i], slabs[i]) for i in range(rows)]
                for i in range(HALO):
                    to_odd[a * HALO + i, part, span] = slabs[i]
                    to_even[a * HALO + i, part, span] = slabs[rows - HALO + i]
                for i in range(rows):
                    mine = (lane >= i * HALO) & (lane < (i + 1) * HALO)
                    if c == 0:
                        lo[t] = jnp.where(mine, move(slabs[i], i * HALO), lo[t])
                    if c == tiles - 1:
                        hi[t] = jnp.where(mine, move(slabs[i], (i + 1) * HALO), hi[t])
        for t in range(2):
            part = slice(t * half, (t + 1) * half)
            left[a, part] = jnp.where(col_odd, hi[t], lo[t])
            right[a, part] = jnp.where(col_odd, lo[t], hi[t])
    for target in (to_odd, to_even):
        target[2 * HALO] = jnp.zeros((depth, cols), jnp.float32)


def corner_kernel(to_odd, to_even, strip_odd, strip_even, odd_out, even_out, *, depth):
    lane = lax.broadcasted_iota(jnp.int32, (depth, LANES), 1)
    first = lane < LANES // 2
    for a in range(2):
        span = slice(a * LANES, (a + 1) * LANES)
        even, odd = strip_even[a], strip_odd[a]
        odd_out[2 * HALO, :, span] = jnp.where(first, even, move(odd, LANES // 2))
        even_out[2 * HALO, :, span] = jnp.where(first, move(even, LANES // 2), odd)


class Field:
    def __init__(self):
        self.where = {}

    def put(self, first, ref, count):
        for i in range(count):
            self.where[first + i] = (ref, i)

    def get(self, j, part):
        ref, i = self.where[j]
        return ref[i, part]

    def set(self, j, part, value):
        ref, i = self.where[j]
        ref[i, part] = value


class Shape:
    def __init__(self, depth, rows, cols):
        flags = self.flags = position()
        self.depth, self.rows, self.cols = depth, rows, cols
        self.half, self.width, self.span = depth // 2, cols + LANES, rows + 2 * HALO
        self.parts = (slice(0, self.half), slice(self.half, depth))
        self.odd, self.col_odd = flags[0] == 1, flags[1] == 1
        self.edge, self.left, self.right = (jnp.where(flags[i], 1.0, 0.0) for i in range(2, 5))
        self.lane = lax.broadcasted_iota(jnp.int32, (self.half, LANES), 1)
        deep = lax.broadcasted_iota(jnp.int32, (self.half, self.width), 0)
        wide = lax.broadcasted_iota(jnp.int32, (self.half, self.width), 1)
        sides = self.left * flag(wide == 0) + self.right * flag(wide == cols - 1)
        self.ends = [sides + flag(deep == 0), sides + flag(deep == self.half - 1)]
        self.x_inner = 1.0 - self.right * flag(wide == cols - 1) - self.left * flag(wide == self.width - 1)
        self.z_inner = flag(deep < self.half - 1)

    def ordered(self, odd, even):
        return jnp.where(self.col_odd, even, odd), jnp.where(self.col_odd, odd, even)

    def side(self, lo, hi, at):
        hi, lo = move(hi, -at * HALO), move(lo, -HALO - at * HALO)
        return jnp.where(self.lane < HALO, hi, jnp.where(self.lane >= LANES - HALO, lo, 0.0))

    def corner(self, message, a, t):
        both = message[2 * HALO, self.parts[t], a * LANES : (a + 1) * LANES]
        return self.ordered(move(both, LANES // 2), both)

    def slab(self, message, a, i, strips, at):
        return [
            jnp.concatenate([message[a * HALO + i, self.parts[t]], self.side(*strips[t], at)], axis=1)
            for t in range(2)
        ]

    def coefficients(self, j, halves, f, own_edge):
        f["kz"].set(j, self.parts[0], halves[0] + halves[1])
        f["kz"].set(j, self.parts[1], (halves[1] + ahead(halves[0], 0)) * self.z_inner)
        for t in range(2):
            f["kx"].set(j, self.parts[t], (halves[t] + ahead(halves[t], 1)) * self.x_inner)
            ends = self.ends[t] + self.edge if own_edge else self.ends[t]
            f["diag"].set(j, self.parts[t], reaction + halves[t] * ends)


def steps():
    middle = (highest + lowest) / 2.0
    spread = (highest - lowest) / 2.0
    sig_ratio = middle / spread
    rho_now = 1.0 / sig_ratio
    for step in range(1, SWEEPS):
        rho_next = 1.0 / (2.0 * sig_ratio - rho_now)
        yield step, rho_next * rho_now, 2.0 * rho_next / spread
        rho_now = rho_next


def apply_rows(sh, f, across, low, high, flux_low, flux_high, emit):
    parts = sh.parts
    for j in range(low, high):
        for t in range(2):
            here = f["dirn"].get(j, parts[t])
            across[j - low, parts[t]] = f["kx"].get(j, parts[t]) * (here - ahead(here, 1))
    here = [f["dirn"].get(low, p) for p in parts]
    flux_y = [f["ky"].get(low - 1, parts[t]) * (f["dirn"].get(low - 1, parts[t]) - here[t]) for t in range(2)]
    if flux_low is not None:
        for t in range(2):
            flux_low(t, flux_y[t])
    for j in range(low, high):
        if j == high - 1 and flux_high is not None:
            nxt, flux = None, [flux_high(t) for t in range(2)]
        else:
            nxt = [f["dirn"].get(j + 1, p) for p in parts]
            flux = [f["ky"].get(j, parts[t]) * (here[t] - nxt[t]) for t in range(2)]
        flux_z0 = f["kz"].get(j, parts[0]) * (here[0] - here[1])
        flux_z1 = f["kz"].get(j, parts[1]) * (here[1] - ahead(here[0], 0))
        along_z = (flux_z0 - back(flux_z1, 0), flux_z1 - flux_z0)
        for t in range(2):
            flux_x = across[j - low, parts[t]]
            applied = (f["diag"].get(j, parts[t]) * here[t] + (flux[t] - flux_y[t])) + along_z[t]
            emit(j, t, here[t], applied + (flux_x - back(flux_x, 1)))
        here, flux_y = nxt, flux


def near_kernel(own_odd, own_even, rows_even, strip_odd, strip_even,
                dirn_a, res_a, pre_a, kx_a, ky_a, kz_a, diag_a, saved, edge_half, image_b, pre_b,
                dirn_b, res_b, kx_b, ky_b, kz_b, diag_b, across, *, depth, rows, cols):
    sh = Shape(depth, rows, cols)
    parts = sh.parts
    mid = 2 * HALO
    f = {name: Field() for name in ("dirn", "res", "pre", "kx", "ky", "kz", "diag")}
    lows = dict(dirn=dirn_a, res=res_a, pre=pre_a, kx=kx_a, ky=ky_a, kz=kz_a, diag=diag_a)
    highs = dict(dirn=dirn_b, res=res_b, pre=pre_b, kx=kx_b, ky=ky_b, kz=kz_b, diag=diag_b)
    for name, field in f.items():
        field.put(HALO, lows[name], HALO)
    for name, ref in highs.items():
        f[name].put(mid, ref, sh.span - mid)
    f["pre"].put(mid, pre_b, HALO + rows - mid)

    def slabs_of(a):
        own = [sh.ordered(strip_odd[a, p], strip_even[a, p]) for p in parts]
        far = [sh.corner(rows_even, a, t) for t in range(2)]
        for i in range(rows):
            message = own_odd if i < HALO else own_even
            yield HALO + i, sh.slab(message, a, i % HALO if i < HALO else i - (rows - HALO), own, i)
        for k in range(HALO):
            yield HALO + rows + k, sh.slab(rows_even, a, HALO - 1 - k, far, HALO - 1 - k)

    middle = (highest + lowest) / 2.0
    for j, slab in slabs_of(0):
        for t in range(2):
            first = slab[t] * (1.0 / middle)
            f["res"].set(j, parts[t], slab[t])
            f["dirn"].set(j, parts[t], first)
            if j < HALO + rows:
                f["pre"].set(j, parts[t], first[:, :cols])
    last = None
    for j, slab in slabs_of(1):
        halves = [0.5 * v for v in slab]
        if last is not None:
            for t in range(2):
                f["ky"].set(j - 1, parts[t], last[t] + halves[t])
        else:
            for t in range(2):
                edge_half[parts[t]] = halves[t]
        if j < sh.span - 1:
            sh.coefficients(j, halves, f, j == HALO)
        last = halves

    for step, keep, gain in steps():

        def emit(j, t, here, applied):
            left_over = f["res"].get(j, parts[t]) - applied
            f["res"].set(j, parts[t], left_over)
            fresh = keep * here + gain * left_over
            f["dirn"].set(j, parts[t], fresh)
            if j < HALO + rows:
                f["pre"].set(j, parts[t], f["pre"].get(j, parts[t]) + fresh[:, :cols])

        def save(t, flux, step=step):
            saved[step - 1, parts[t]] = flux

        apply_rows(sh, f, across, HALO + step, sh.span - step, save, None, emit)

    def finish(j, t, here, applied):
        start = own_even[j - mid, parts[t]]
        image_b[j - mid, parts[t]] = start - (f["res"].get(j, parts[t])[:, :cols] - applied[:, :cols])

    def save_last(t, flux):
        saved[SWEEPS - 1, parts[t]] = flux

    apply_rows(sh, f, across, HALO + SWEEPS, HALO + rows, save_last, None, finish)


def split(x):
    high = x.astype(jnp.bfloat16)
    return high, (x - high.astype(jnp.float32)).astype(jnp.bfloat16)


def far_kernel(rows_odd, own_odd, dirn_a, res_a, pre_a, kx_a, ky_a, kz_a, diag_a, saved, edge_half, image_b, pre_b,
               signs_hbm, picks_hbm, mix_hbm, image, pre, sketch_out,
               dirn, res, kx, ky, kz, diag, across, flip_high, flip_low, signs, picks, mix, sems, *, depth, rows, cols, samples):
    loads = [
        pltpu.make_async_copy(signs_hbm, signs, sems.at[0]),
        pltpu.make_async_copy(picks_hbm, picks, sems.at[1]),
        pltpu.make_async_copy(mix_hbm, mix, sems.at[2]),
    ]
    for load in loads:
        load.start()
    sh = Shape(depth, rows, cols)
    parts = sh.parts
    f = {name: Field() for name in ("dirn", "res", "pre", "kx", "ky", "kz", "diag")}
    mine = dict(dirn=dirn, res=res, kx=kx, ky=ky, kz=kz, diag=diag)
    given = dict(dirn=dirn_a, res=res_a, pre=pre_a, kx=kx_a, ky=ky_a, kz=kz_a, diag=diag_a)
    for name, field in f.items():
        if name in mine:
            field.put(0, mine[name], HALO)
        field.put(HALO, given[name], HALO)
    middle = (highest + lowest) / 2.0
    corners = [[sh.corner(rows_odd, a, t) for t in range(2)] for a in range(2)]
    last = None
    for k in reversed(range(HALO)):
        j = HALO - 1 - k
        slab = sh.slab(rows_odd, 0, k, corners[0], k)
        for t in range(2):
            f["res"].set(j, parts[t], slab[t])
            f["dirn"].set(j, parts[t], slab[t] * (1.0 / middle))
        halves = [0.5 * v for v in sh.slab(rows_odd, 1, k, corners[1], k)]
        if last is not None:
            for t in range(2):
                f["ky"].set(j - 1, parts[t], last[t] + halves[t])
        if j > 0:
            sh.coefficients(j, halves, f, False)
        last = halves
    for t in range(2):
        f["ky"].set(HALO - 1, parts[t], (last[t] + edge_half[parts[t]]) * (1.0 - sh.edge))

    def hand_over(j, t):
        if j >= HALO and t == 1:
            f["dirn"].where[j] = (dirn, j)
            f["res"].where[j] = (res, j)
            f["pre"].where[j] = (pre, j - HALO)

    for step, keep, gain in steps():

        def emit(j, t, here, applied):
            left_over = f["res"].get(j, parts[t]) - applied
            fresh = keep * here + gain * left_over
            at = parts[t]
            res[j, at] = left_over
            dirn[j, at] = fresh
            if j >= HALO:
                pre[j - HALO, at] = f["pre"].get(j, at) + fresh[:, :cols]
            hand_over(j, t)

        apply_rows(sh, f, across, step, HALO + step, None, lambda t, step=step: saved[step - 1, parts[t]], emit)

    def finish(j, t, here, applied):
        start = own_odd[j - HALO, parts[t]]
        image[j - HALO, parts[t]] = start - (f["res"].get(j, parts[t])[:, :cols] - applied[:, :cols])

    apply_rows(sh, f, across, HALO, 2 * HALO, None, lambda t: saved[SWEEPS - 1, parts[t]], finish)
    for i in range(rows):
        if i >= HALO:
            image[i] = image_b[i - HALO]
            pre[i] = pre_b[i - HALO]
        elif f["pre"].where[HALO + i][0] is not pre:
            pre[i] = pre_a[i]
    for load in loads:
        load.wait()
    for r in range(rows):
        flipped = image[r + sh.flags[0] * (rows - 1 - 2 * r)] * signs[r : r + 1, :].astype(jnp.float32)
        at = slice(r * depth, (r + 1) * depth)
        flip_high[at], flip_low[at] = split(flipped)

    def dot(a, b, dims):
        return lax.dot_general(a, b, (dims, ((), ())), preferred_element_type=jnp.float32)

    col_ids = lax.broadcasted_iota(jnp.int32, (samples, cols), 1)
    sample_ids = lax.broadcasted_iota(jnp.int32, (samples, cols), 0)
    wanted = jnp.zeros((samples, cols), jnp.int32)
    for n in range(samples):
        wanted = jnp.where(sample_ids == n, picks[n], wanted)
    chosen = flag(wanted == col_ids).astype(jnp.bfloat16)
    picked = dot(chosen, flip_high[...], ((1,), (1,))) + dot(chosen, flip_low[...], ((1,), (1,)))
    high, low = split(picked)
    rest = dot(high, mix[1], ((1,), (0,))) + dot(low, mix[0], ((1,), (0,)))
    sketch_out[...] = dot(high, mix[0], ((1,), (0,))) + rest


def tail_kernel(pre, image, precond_out, image_out, *, depth, rows, cols):
    half = depth // 2
    flags = position()
    for c in range(cols // LANES):
        span = slice(c * LANES, (c + 1) * LANES)
        for r in range(0, rows, half):
            for t in range(2):
                part = slice(t * half, (t + 1) * half)
                for source, target in ((pre, precond_out), (image, image_out)):
                    found = [source[r + i + flags[0] * (rows - 1 - 2 * (r + i)), part, span] for i in range(half)]
                    for s, tile in enumerate(turn(found)):
                        target[2 * s + t, r : r + half, span] = tile


def in_hbm(array):
    return pltpu.with_memory_space_constraint(array, pltpu.HBM)


def whole_step(basis_vec, conductivity, sign_vals, sample_cols):
    depth, rows, cols = basis_vec.shape
    samples = sample_cols.shape[0]
    assert depth == 16 and rows == 2 * HALO and cols == 2 * LANES
    gx_size, gy_size = lax.axis_size("gx"), lax.axis_size("gy")
    gx_index = lax.axis_index("gx")
    vmem, hbm = (pl.BlockSpec(memory_space=space) for space in (pltpu.VMEM, pltpu.HBM))
    f32 = jnp.float32
    sizes = dict(depth=depth, rows=rows, cols=cols)
    width, span, mid = cols + LANES, rows + 2 * HALO, 2 * HALO
    wide = lambda n: jax.ShapeDtypeStruct((n, depth, width), f32)
    slim = lambda n: jax.ShapeDtypeStruct((n, depth, cols), f32)
    wide_scratch = lambda n: pltpu.VMEM((n, depth, width), f32)
    small = lambda mib: pltpu.CompilerParams(vmem_limit_bytes=mib << 20)
    message = slim(2 * HALO + 1)
    strip = jax.ShapeDtypeStruct((2, depth, LANES), f32)
    own_odd, own_even, strip_to_odd, strip_to_even = pl.pallas_call(
        lambda *refs: pack_kernel(*refs, **sizes),
        in_specs=[hbm] * 2,
        out_specs=[vmem] * 4,
        out_shape=[message, message, strip, strip],
        scratch_shapes=[
            pltpu.VMEM((2, cols // LANES, depth, rows, LANES), f32),
            pltpu.SemaphoreType.DMA((2, cols // LANES)),
        ],
        compiler_params=small(4),
        name="pack",
    )(in_hbm(basis_vec), in_hbm(conductivity))
    strip_even = exchange(strip_to_even, same, even_pair)
    strip_odd = exchange(strip_to_odd, same, odd_pair)
    own_odd, own_even = pl.pallas_call(
        lambda *refs: corner_kernel(*refs, depth=depth),
        in_specs=[vmem] * 4,
        out_specs=[vmem] * 2,
        out_shape=[message, message],
        input_output_aliases={0: 0, 1: 1},
        compiler_params=small(4),
        name="corners",
    )(own_odd, own_even, strip_odd, strip_even)
    rows_odd = exchange(own_odd, odd_pair, same)
    rows_even = exchange(own_even, even_pair, same)
    *handed, image_b, pre_b = pl.pallas_call(
        lambda *refs: near_kernel(*refs, **sizes),
        in_specs=[vmem] * 5,
        out_specs=[vmem] * 11,
        out_shape=[wide(HALO), wide(HALO), slim(HALO), wide(HALO), wide(HALO), wide(HALO), wide(HALO), wide(SWEEPS),
                   jax.ShapeDtypeStruct((depth, width), f32), slim(rows - HALO), slim(rows - HALO)],
        scratch_shapes=[wide_scratch(span - mid)] * 6 + [wide_scratch(span - HALO)],
        compiler_params=small(16),
        name="near",
    )(own_odd, own_even, rows_even, strip_odd, strip_even)
    mix = hartley_mix(depth, rows, 1.0 / np.sqrt(gx_size))
    mix_high = mix.astype(jnp.bfloat16)
    mix = jnp.asarray(np.stack([mix_high, (mix - mix_high.astype(np.float32)).astype(jnp.bfloat16)]))
    image, pre, current = pl.pallas_call(
        lambda *refs: far_kernel(*refs, samples=samples, **sizes),
        in_specs=[vmem] * 13 + [hbm] * 3,
        out_specs=[vmem] * 3,
        out_shape=[slim(rows), slim(rows), jax.ShapeDtypeStruct((samples, depth * rows), f32)],
        scratch_shapes=[wide_scratch(mid)] * 2 + [wide_scratch(HALO)] * 5
        + [pltpu.VMEM((depth * rows, cols), jnp.bfloat16)] * 2
        + [pltpu.VMEM((rows, cols), jnp.int32), pltpu.SMEM((samples,), jnp.int32)]
        + [pltpu.VMEM(mix.shape, jnp.bfloat16), pltpu.SemaphoreType.DMA((3,))],
        compiler_params=small(16),
        name="far",
    )(rows_odd, own_odd, *handed, image_b, pre_b, in_hbm(sign_vals), in_hbm(sample_cols), in_hbm(mix))
    precond_out, image_out = pl.pallas_call(
        lambda *refs: tail_kernel(*refs, **sizes),
        in_specs=[vmem] * 2,
        out_specs=[vmem] * 2,
        out_shape=[jax.ShapeDtypeStruct((depth, rows, cols), f32)] * 2,
        compiler_params=small(8),
        name="tail",
    )(pre, image)
    gx_bits = gx_size.bit_length() - 1
    for group in [[0]] + bit_groups(list(range(1, gx_bits))):
        total = walsh_sign(gx_index, 0, group) * current
        for mask in masks_of(group)[1:]:
            total = total + walsh_sign(gx_index, mask, group) * swap(current, "gx", mask)
        current = total
    for group in bit_groups(list(range(gy_size.bit_length() - 1))):
        current = current + sum(swap(current, "gy", mask) for mask in masks_of(group)[1:])
    return precond_out, image_out, current.T.reshape(depth, rows, samples)


def solution(mesh):
    in_specs = (P(None, "gx", "gy"), P(None, "gx", "gy"), P("gx", "gy"), P("gy"))
    out_specs = (P(None, "gx", "gy"), P(None, "gx", "gy"), P(None, "gx", None))
    return jax.shard_map(whole_step, mesh=mesh, in_specs=in_specs, out_specs=out_specs, check_vma=False)
```
